512 devices in a mesh: gx: 32 (over y, x), gz: 16 (over z, core).
Axes of the slice: x: 4, y: 8, z: 8, core: 2. Of those that a mesh axis runs over, the one named last changes fastest.
Arguments:
- factor: float32 [3, 256, 4, 128, 256], P(None, 'gz', None, 'gx'), may hold values from -6 to 6
- gain: float32 [3, 256, 4, 128, 256], P(None, 'gz', None, 'gx'), may hold values from -6 to 6
- base_flow: float32 [256, 128, 256], P('gz', 'gx'), may hold values from 0.25 to 2
- shift_index: int32 [1], replicated, may hold values from 0 to 7
- sensor_cells: int32 [4, 4], replicated, may hold values from 0 to 255, as said below
Outputs:
- new_factor: float32 [3, 256, 4, 128, 256], P(None, 'gz', None, 'gx')
- new_gain: float32 [3, 256, 4, 128, 256], P(None, 'gz', None, 'gx')
- gram: float32 [4, 4], replicated
The draws below stay inside these ranges and needn't reach their ends.
Inputs may be any that keep to these rules, and one draw needn't show every extreme that they name: `sensor_cells`: row i gives sensor i's velocity component (0 to 2), spanwise index (0 to 255), streamwise index (0 to 127) and wall-normal index (0 to 255); in every draw some sensor sits at spanwise index 255, some at streamwise index 127 and some at wall-normal index 255.
All inputs are finite; a program needn't handle non-finite values.
Results may differ from the reference program's by a relative error of at most 0.03.
Values sent between devices are 32-bit elements; how exact they have to be, the bound alone decides.
A program may use at most 64 MiB of HBM per device.

```python
import math
import jax
import jax.numpy as jnp
from jax import lax

COLS = 4
NZ = 256
NY = 256
SWEEPS = 3
POISSON = 4
SHIFTS = 8
NX = 128


def draw_sensor_cells(key, part):
    subkeys = jax.random.split(key, 7)
    rows = jnp.arange(COLS)
    component = jax.random.randint(subkeys[0], (COLS,), 0, 3)
    spanwise = jax.random.randint(subkeys[1], (COLS,), 0, NZ)
    streamwise = jax.random.randint(subkeys[2], (COLS,), 0, NX)
    normal = jax.random.randint(subkeys[3], (COLS,), 0, NY)
    span_row = jax.random.randint(subkeys[4], (), 0, COLS)
    stream_row = jax.random.randint(subkeys[5], (), 0, COLS)
    normal_row = jax.random.randint(subkeys[6], (), 0, COLS)
    spanwise = jnp.where(rows == span_row, NZ - 1, spanwise)
    streamwise = jnp.where(rows == stream_row, NX - 1, streamwise)
    normal = jnp.where(rows == normal_row, NY - 1, normal)
    return jnp.stack([component, spanwise, streamwise, normal], axis=1).astype(jnp.int32)


def block_levels(stream_key, dims, cuts, smallest, top_value):
    level = 1.0
    for dim, blocks in cuts:
        steps = jax.random.uniform(jax.random.fold_in(jax.random.fold_in(stream_key, 6), dim), (blocks,), jnp.float32, smallest / len(cuts), top_value / len(cuts))
        level = level * jnp.repeat(jnp.exp(steps), dims[dim] // blocks).reshape((-1,) + (1,) * (len(dims) - 1 - dim))
    return level


def normal_values(own_key, dims, deviation, most, pieces=(), kind=jnp.bfloat16):
    entries = deviation * jax.random.normal(own_key, dims, jnp.float32)
    if pieces:
        entries = entries * block_levels(own_key, dims, pieces, -0.22, 0.18)
    return jnp.clip(entries, -most, most).astype(kind)


def setup_inputs(seed: int = 0) -> dict:
    key_list = jax.random.split(jax.random.key(seed), 6)
    return {
        "factor": normal_values(key_list[0], (3, NZ, COLS, NX, NY), 1.0, 6.0, ((1, 16), (3, 32)), jnp.float32),
        "gain": normal_values(key_list[1], (3, NZ, COLS, NX, NY), 1.0, 6.0, ((1, 16), (3, 32)), jnp.float32),
        "base_flow": jnp.clip(jnp.exp(math.log(2.0) - 2.0794415 * jax.random.uniform(key_list[2], (NZ, NX, NY), jnp.float32) ** block_levels(key_list[2], (NZ, NX, NY), ((0, 16), (1, 32)), -0.2, 0.2)), 0.25, 2.0),
        "shift_index": jax.random.randint(key_list[3], (1,), 0, SHIFTS).astype(jnp.int32),
        "sensor_cells": draw_sensor_cells(jax.random.fold_in(key_list[5], 71), 0),
    }


viscosity = 0.4
shift_table = (0.6, 0.8, 1.0, 1.25, 1.6, 2.0, 2.5, 3.2)
chebyshev_weights = (1.0 / 1.9352976, 1.0 / 1.4752809, 1.0 / 0.8247191, 1.0 / 0.3647024)
highest = lax.Precision.HIGHEST

def neighbours(grid_field):
    padded = jnp.pad(grid_field, ((0, 0), (0, 0), (0, 0), (1, 1), (1, 1)))
    summed = padded[:, :, :, 2:, 1:-1] + padded[:, :, :, :-2, 1:-1]
    summed = summed + padded[:, :, :, 1:-1, 2:] + padded[:, :, :, 1:-1, :-2]
    summed = summed + jnp.roll(grid_field, 1, axis=1) + jnp.roll(grid_field, -1, axis=1)
    return (summed, padded[:, :, :, :-2, 1:-1])

def hartley(grid_field):
    spectrum = jnp.fft.fft(grid_field, axis=0)
    return (jnp.real(spectrum) - jnp.imag(spectrum)) / math.sqrt(NZ)

def reference(factor, gain, base_flow, shift_index, sensor_cells):
    shift_value = jnp.asarray(shift_table, jnp.float32)[shift_index[0]]
    base_field = base_flow[None, :, None, :, :]
    diagonal = shift_value + 6.0 * viscosity + base_field
    source = -factor
    velocity = source / diagonal
    for sweep_index in range(SWEEPS):
        beside_all, behind = neighbours(velocity)
        velocity = (source + viscosity * beside_all + base_field * behind) / diagonal
    stream = velocity[0]
    normal = velocity[1]
    spanwise = velocity[2]
    divergence = 2.0 * (stream - jnp.pad(stream, ((0, 0), (0, 0), (1, 0), (0, 0)))[:, :, :-1, :])
    divergence = divergence + (normal - jnp.pad(normal, ((0, 0), (0, 0), (0, 0), (1, 0)))[:, :, :, :-1])
    divergence = divergence + (spanwise - jnp.roll(spanwise, 1, axis=0))
    modes_rhs = -hartley(divergence)
    wavenumber = 2.0 * math.pi * jnp.arange(NZ).astype(jnp.float32) / NZ
    mode_diagonal = (10.0 + (2.0 - 2.0 * jnp.cos(wavenumber)))[:, None, None, None]
    pressure = chebyshev_weights[0] * modes_rhs / mode_diagonal
    for sweep_level in range(1, POISSON):
        padded = jnp.pad(pressure, ((0, 0), (0, 0), (1, 1), (1, 1)))
        beside_all = 4.0 * (padded[:, :, 2:, 1:-1] + padded[:, :, :-2, 1:-1]) + padded[:, :, 1:-1, 2:] + padded[:, :, 1:-1, :-2]
        pressure = pressure + chebyshev_weights[sweep_level] * (modes_rhs - (mode_diagonal * pressure - beside_all)) / mode_diagonal
    pressure = hartley(pressure)
    padded = jnp.pad(pressure, ((0, 0), (0, 0), (0, 1), (0, 1)))
    gradient = jnp.stack([2.0 * (padded[:, :, 1:, :-1] - pressure), padded[:, :, :-1, 1:] - pressure, jnp.roll(pressure, -1, axis=0) - pressure])
    solved = velocity - gradient
    new_factor = factor + 2.0 * shift_value * solved
    readout = solved[sensor_cells[:, 0], sensor_cells[:, 1], :, sensor_cells[:, 2], sensor_cells[:, 3]]
    new_gain = gain + 2.0 * shift_value * jnp.einsum('czjxy,ij->czixy', solved, readout, precision=highest)
    gram = jnp.einsum('czixy,czjxy->ij', new_factor, new_factor, precision=highest) / (3.0 * NX * NY * NZ)
    return (new_factor, new_gain, gram)
```

```python
import functools
import math

import jax
import jax.numpy as jnp
from jax import lax
from jax.experimental import pallas as pl
from jax.experimental.pallas import tpu as pltpu
from jax.sharding import PartitionSpec as P

SWEEPS = 3
POISSON = 4
SHIFTS = 8


viscosity = 0.4
shift_table = (0.6, 0.8, 1.0, 1.25, 1.6, 2.0, 2.5, 3.2)
chebyshev_weights = (1.0 / 1.9352976, 1.0 / 1.4752809, 1.0 / 0.8247191, 1.0 / 0.3647024)
highest = lax.Precision.HIGHEST


def padded_2(cells, sides, width, closed):
    for axis, dim in sides:
        count = lax.axis_size(axis)
        ends = count if closed else count - 1
        head = lax.slice_in_dim(cells, 0, width, axis=dim)
        tail = lax.slice_in_dim(cells, cells.shape[dim] - width, cells.shape[dim], axis=dim)
        cells = jnp.concatenate(
            [
                lax.ppermute(tail, axis, [(i, (i + 1) % count) for i in range(ends)]),
                cells,
                lax.ppermute(head, axis, [((i + 1) % count, i) for i in range(ends)]),
            ],
            axis=dim,
        )
    return cells


def around_sum(padded):
    summed = padded[:, 1:-1, :, 2:, 1:-1] + padded[:, 1:-1, :, :-2, 1:-1]
    summed = summed + padded[:, 1:-1, :, 1:-1, 2:] + padded[:, 1:-1, :, 1:-1, :-2]
    return summed + padded[:, 2:, :, 1:-1, 1:-1] + padded[:, :-2, :, 1:-1, 1:-1]


def sum_kernel(sizes, tile_ref, out_ref, slots_z, slots_x, slots_y, mid, sends, recvs):
    count_z, count_x, count_y = sizes
    gx, gz = lax.axis_index("gx"), lax.axis_index("gz")
    here_x, here_y = gx % count_x, gx // count_x

    def partner(stage, offset):
        if stage == 0:
            return (gx, (gz + offset) % count_z)
        if stage == 1:
            return (here_y * count_x + (here_x + offset) % count_x, gz)
        return ((here_y + offset) % count_y * count_x + here_x, gz)

    counts = (count_z, count_x, count_y)
    barrier = pltpu.get_barrier_semaphore()
    for stage in range(3):
        def greet(offset, carry, stage=stage):
            pl.semaphore_signal(
                barrier, inc=1, device_id=partner(stage, offset), device_id_type=pl.DeviceIdType.MESH
            )
            return carry

        lax.fori_loop(1, counts[stage], greet, 0)
    pl.semaphore_wait(barrier, sum(counts) - 3)
    places = (gz, here_x, here_y)
    bases = (0, count_z, count_z + count_x)
    source = tile_ref
    for stage, slots in enumerate((slots_z, slots_x, slots_y)):
        base = bases[stage]

        def copy(offset, stage=stage, slots=slots, base=base, source=source):
            return pltpu.make_async_remote_copy(
                src_ref=source,
                dst_ref=slots.at[places[stage]],
                send_sem=sends.at[base + offset],
                recv_sem=recvs.at[base + offset],
                device_id=partner(stage, offset),
                device_id_type=pl.DeviceIdType.MESH,
            )

        def start(offset, carry, copy=copy):
            copy(offset).start()
            return carry

        def finish(offset, carry, copy=copy):
            copy(offset).wait()
            return carry

        lax.fori_loop(1, counts[stage], start, 0)
        slots[places[stage]] = source[...]
        lax.fori_loop(1, counts[stage], finish, 0)
        total = slots[0]
        for place in range(1, counts[stage]):
            total = total + slots[place]
        if stage < 2:
            mid[stage] = total
            source = mid.at[stage]
        else:
            out_ref[...] = total


def sum_all(tile, sizes):
    count = sum(sizes)
    return pl.pallas_call(
        functools.partial(sum_kernel, sizes),
        out_shape=jax.ShapeDtypeStruct((8, 128), jnp.float32),
        in_specs=[pl.BlockSpec(memory_space=pltpu.VMEM)],
        out_specs=pl.BlockSpec(memory_space=pltpu.VMEM),
        scratch_shapes=[pltpu.VMEM((size, 8, 128), jnp.float32) for size in sizes]
        + [
            pltpu.VMEM((2, 8, 128), jnp.float32),
            pltpu.SemaphoreType.DMA((count,)),
            pltpu.SemaphoreType.DMA((count,)),
        ],
        compiler_params=pltpu.CompilerParams(collective_id=0, has_side_effects=True),
        name="sum_all",
    )(tile)


def shards(factor, gain, base_flow, shift_index, sensor_cells):
    components, span_cells, columns, stream_cells, normal_cells = factor.shape
    stream_start = lax.axis_index("gx") * stream_cells
    span_start = lax.axis_index("gz") * span_cells
    stream_total = stream_cells * lax.axis_size("gx")
    span_total = span_cells * lax.axis_size("gz")
    shift_values = jnp.asarray(shift_table, jnp.float32)
    shift_value = jnp.sum(jnp.where(jnp.arange(SHIFTS) == shift_index[0], shift_values, 0.0))
    base_field = base_flow[None, :, None, :, :]
    diagonal = shift_value + 6.0 * viscosity + base_field
    source = -factor

    def stream_inside(extent, margin):
        positions = stream_start - margin + jnp.arange(extent)
        return ((positions >= 0) & (positions < stream_total)).astype(jnp.float32)

    def extend(grid_field):
        padded = padded_2(grid_field, (("gx", 3), ("gz", 1)), 1, True)
        padded = padded * stream_inside(stream_cells + 2, 1)[None, None, None, :, None]
        return jnp.pad(padded, ((0, 0), (0, 0), (0, 0), (0, 0), (1, 1)))

    velocity = source / diagonal
    for sweep_index in range(SWEEPS):
        padded = extend(velocity)
        velocity = (
            source + viscosity * around_sum(padded) + base_field * padded[:, 1:-1, :, :-2, 1:-1]
        ) / diagonal
    padded = extend(velocity)
    divergence = 2.0 * (velocity[0] - padded[0, 1:-1, :, :-2, 1:-1])
    divergence = divergence + (velocity[1] - padded[1, 1:-1, :, 1:-1, :-2])
    divergence = divergence + (velocity[2] - padded[2, :-2, :, 1:-1, 1:-1])
    span_index = jnp.arange(span_total)
    products = span_index[:, None] * span_index[None, :] % span_total
    angles = 2.0 * math.pi * products.astype(jnp.float32) / span_total
    hartley_table = (jnp.cos(angles) + jnp.sin(angles)) / math.sqrt(span_total)

    def turn_modes(exchanged):
        turned = jnp.einsum("kz,zay->kay", hartley_table, exchanged, precision=highest)
        return lax.all_to_all(turned, "gz", split_axis=0, concat_axis=1, tiled=True)

    def transform(grid_field):
        flat = grid_field.reshape(span_cells, columns * stream_cells, normal_cells)
        result = turn_modes(lax.all_to_all(flat, "gz", split_axis=1, concat_axis=0, tiled=True))
        return result.reshape(span_cells, columns, stream_cells, normal_cells)

    modes_rhs = -transform(divergence)
    wave_index = span_start + jnp.arange(span_cells)
    wavenumber = 2.0 * math.pi * wave_index.astype(jnp.float32) / span_total
    mode_diagonal = (10.0 + (2.0 - 2.0 * jnp.cos(wavenumber)))[:, None, None, None]
    pressure = chebyshev_weights[0] * modes_rhs / mode_diagonal
    for sweep_level in range(1, POISSON):
        padded = padded_2(pressure, (("gx", 2),), 1, False)
        padded = jnp.pad(padded, ((0, 0), (0, 0), (0, 0), (1, 1)))
        beside_all = (
            4.0 * (padded[:, :, 2:, 1:-1] + padded[:, :, :-2, 1:-1])
            + padded[:, :, 1:-1, 2:]
            + padded[:, :, 1:-1, :-2]
        )
        pressure = (
            pressure
            + chebyshev_weights[sweep_level]
            * (modes_rhs - (mode_diagonal * pressure - beside_all))
            / mode_diagonal
        )
    pressure = transform(pressure)
    padded = extend(pressure[None])[0]
    gradient = jnp.stack(
        [
            2.0 * (padded[1:-1, :, 2:, 1:-1] - pressure),
            padded[1:-1, :, 1:-1, 2:] - pressure,
            padded[2:, :, 1:-1, 1:-1] - pressure,
        ]
    )
    solved = velocity - gradient
    span_ids = span_start + jnp.arange(span_cells)
    stream_ids = stream_start + jnp.arange(stream_cells)
    normal_ids = jnp.arange(normal_cells)
    located = span_ids[None, :, None, None] == sensor_cells[:, 1][:, None, None, None]
    located = located & (stream_ids[None, None, :, None] == sensor_cells[:, 2][:, None, None, None])
    located = located & (normal_ids[None, None, None, :] == sensor_cells[:, 3][:, None, None, None])
    picked = jnp.einsum("szxy,czjxy->scj", located.astype(jnp.float32), solved, precision=highest)
    chooser = (jnp.arange(3)[None, :] == sensor_cells[:, 0:1]).astype(jnp.float32)
    readout_local = jnp.sum(picked * chooser[:, :, None], axis=1)
    new_factor = factor + 2.0 * shift_value * solved
    gram_local = jnp.einsum("czixy,czjxy->ij", new_factor, new_factor, precision=highest)
    tile = jnp.pad(jnp.concatenate([gram_local, readout_local]), ((0, 0), (0, 124)))
    count_gx = lax.axis_size("gx")
    tile = sum_all(tile, (lax.axis_size("gz"), 4, count_gx // 4))
    gram_total, readout = tile[:4, :4], tile[4:8, :4]
    gram = gram_total / (3.0 * stream_total * normal_cells * span_total)
    new_gain = gain + 2.0 * shift_value * jnp.einsum(
        "czjxy,ij->czixy", solved, readout, precision=highest
    )
    return (new_factor, new_gain, gram)


def solution(mesh):
    placed = (
        P(None, "gz", None, "gx", None),
        P(None, "gz", None, "gx", None),
        P("gz", "gx", None),
        P(),
        P(),
    )
    return jax.shard_map(
        shards,
        mesh=mesh,
        in_specs=placed,
        out_specs=(P(None, "gz", None, "gx", None), P(None, "gz", None, "gx", None), P()),
        check_vma=False,
    )
```

```python
import functools
import math

import jax
import jax.numpy as jnp
import numpy as np
from jax import lax
from jax.experimental import pallas as pl
from jax.experimental.pallas import tpu as pltpu
from jax.sharding import PartitionSpec as P

SWEEPS = 3
POISSON = 4
SHIFTS = 8


viscosity = 0.4
shift_table = (0.6, 0.8, 1.0, 1.25, 1.6, 2.0, 2.5, 3.2)
chebyshev_weights = (1.0 / 1.9352976, 1.0 / 1.4752809, 1.0 / 0.8247191, 1.0 / 0.3647024)
highest = lax.Precision.HIGHEST


def step_kernel(
    sizes,
    shift_ref,
    cells_ref,
    factor_ref,
    base_ref,
    table_ref,
    scale_ref,
    solved_ref,
    out_ref,
    fields,
    inverse,
    row_sends,
    row_halos,
    blocks,
    planes,
    rhs,
    modes,
    beside,
    pressure,
    pressure_row,
    pressure_halo,
    slots_z,
    slots_x,
    slots_y,
    mid,
    halo_send,
    halo_recv,
    turn_send,
    turn_recv,
    mode_send,
    mode_recv,
    sum_send,
    sum_recv,
):
    count_z, count_x, count_y = sizes
    count_gx = count_x * count_y
    components, stream_cells, columns, span_cells, normal_cells = factor_ref.shape
    last_cell = stream_cells - 1
    cells = stream_cells * columns
    gx, gz = lax.axis_index("gx"), lax.axis_index("gz")
    here_x, here_y = gx % count_x, gx // count_x
    next_gx = ((gx + 1) % count_gx, gz)
    before_gx = ((gx + count_gx - 1) % count_gx, gz)
    next_gz = (gx, (gz + 1) % count_z)
    before_gz = (gx, (gz + count_z - 1) % count_z)
    shift = shift_ref[0]

    odd = gx % 2
    turn = 1 - 2 * odd

    def mirrored(cell):
        return odd * last_cell + turn * cell

    plane_cell = mirrored(gz % stream_cells)
    plane_column = gz // stream_cells
    at_end = plane_cell // last_cell
    at_start = (last_cell - plane_cell) // last_cell
    plane_next = ((gx + at_end) % count_gx, gz + turn * (1 - at_end))
    plane_before = ((gx + count_gx - at_start) % count_gx, gz - turn * (1 - at_start))

    def low(cell):
        return jnp.where(gx + cell == 0, 0.0, 1.0)

    def high(cell):
        return jnp.where(count_gx - 1 - gx + last_cell - cell == 0, 0.0, 1.0)

    def partner(stage, offset):
        if stage == 0:
            return (gx, (gz + offset) % count_z)
        if stage == 1:
            return (here_y * count_x + (here_x + offset) % count_x, gz)
        return ((here_y + offset) % count_y * count_x + here_x, gz)

    def remote(src, dst, send, recv, device):
        return pltpu.make_async_remote_copy(
            src_ref=src,
            dst_ref=dst,
            send_sem=send,
            recv_sem=recv,
            device_id=device,
            device_id_type=pl.DeviceIdType.MESH,
        )

    def loop(first, end, act):
        def run(index, carry):
            act(index)
            return carry

        lax.fori_loop(first, end, run, 0)

    counts = (count_z, count_x, count_y)
    barrier = pltpu.get_barrier_semaphore()

    def greet(device):
        pl.semaphore_signal(barrier, inc=1, device_id=device, device_id_type=pl.DeviceIdType.MESH)

    for stage in range(3):
        loop(1, counts[stage], lambda offset, stage=stage: greet(partner(stage, offset)))
    greet(next_gx)
    greet(before_gx)

    rows = lax.broadcasted_iota(jnp.int32, (span_cells, normal_cells), 0)
    lanes = lax.broadcasted_iota(jnp.int32, (span_cells, normal_cells), 1)

    def normal_before(block):
        return jnp.where(lanes == 0, 0.0, pltpu.roll(block, 1, 1))

    def normal_after(block):
        return jnp.where(lanes == normal_cells - 1, 0.0, pltpu.roll(block, normal_cells - 1, 1))

    def span_before(block, halo):
        return jnp.where(rows == 0, halo, pltpu.roll(block, 1, 0))

    def span_after(block, halo):
        return jnp.where(rows == span_cells - 1, halo, pltpu.roll(block, span_cells - 1, 0))

    def halo_copies(level, part):
        moves = (
            (fields.at[level, part, stream_cells], fields.at[level, part, 0], next_gx),
            (fields.at[level, part, 1], fields.at[level, part, stream_cells + 1], before_gx),
            (row_sends.at[level, part, 0], row_halos.at[level, part, 0], next_gz),
            (row_sends.at[level, part, 1], row_halos.at[level, part, 1], before_gz),
        )
        sides = (0, 1, 2, 3) if level < SWEEPS else ((0,), (), (2,))[part]
        copies = []
        for side in sides:
            src, dst, device = moves[side]
            copies.append(
                remote(src, dst, halo_send.at[level, part, side], halo_recv.at[level, part, side], device)
            )
        return copies

    def keep(level, part, index, block):
        cell, column = lax.div(index, columns), lax.rem(index, columns)
        fields[level, part, cell + 1, column] = block
        row_sends[level, part, 0, index] = block[span_cells - 1 :]
        row_sends[level, part, 1, index] = block[:1]

    def invert(cell):
        inverse[cell] = 1.0 / (shift + 6.0 * viscosity + base_ref[cell])

    loop(0, stream_cells, invert)
    for part in range(components):
        def first_guess(index, part=part):
            cell, column = lax.div(index, columns), lax.rem(index, columns)
            keep(0, part, index, -factor_ref[part, cell, column] * inverse[cell])

        loop(0, cells, first_guess)
        if part == 0:
            pl.semaphore_wait(barrier, sum(counts) - 3 + 2)
        for copy in halo_copies(0, part):
            copy.start()
    for level in range(SWEEPS):
        for part in range(components):
            for copy in halo_copies(level, part):
                copy.wait()

            def sweep(index, level=level, part=part):
                cell, column = lax.div(index, columns), lax.rem(index, columns)
                block = fields[level, part, cell + 1, column]
                behind = fields[level, part, cell, column] * low(cell)
                around = behind + fields[level, part, cell + 2, column] * high(cell)
                around = around + normal_before(block) + normal_after(block)
                around = around + span_before(block, row_halos[level, part, 0, index])
                around = around + span_after(block, row_halos[level, part, 1, index])
                total = viscosity * around + base_ref[cell] * behind - factor_ref[part, cell, column]
                keep(level + 1, part, index, total * inverse[cell])

            loop(0, cells, sweep)
            for copy in halo_copies(level + 1, part):
                copy.start()
    for part in range(components):
        for copy in halo_copies(SWEEPS, part):
            copy.wait()

    def diverge(index):
        cell, column = lax.div(index, columns), lax.rem(index, columns)
        normal = fields[SWEEPS, 1, cell + 1, column]
        span = fields[SWEEPS, 2, cell + 1, column]
        total = 2.0 * (
            fields[SWEEPS, 0, cell + 1, column] - fields[SWEEPS, 0, cell, column] * low(cell)
        )
        total = total + (normal - normal_before(normal))
        total = total + (span - span_before(span, row_halos[SWEEPS, 2, 0, index]))
        blocks[column * stream_cells + mirrored(cell)] = -total

    loop(0, cells, diverge)

    def gather_copy(offset):
        device = partner(0, offset)
        return remote(
            blocks.at[device[1]], planes.at[gz], turn_send.at[0, offset], turn_recv.at[0, offset], device
        )

    loop(1, count_z, lambda offset: gather_copy(offset).start())
    planes[gz] = blocks[gz]
    loop(1, count_z, lambda offset: gather_copy(offset).wait())
    span_total = count_z * span_cells
    whole = planes[...].reshape(span_total, normal_cells)
    spectrum = jnp.dot(
        table_ref[...], whole, precision=highest, preferred_element_type=jnp.float32
    ) * scale_ref[...]
    shape = (count_z, span_cells, normal_cells)
    rhs[...] = spectrum.reshape(shape)
    modes[0] = (chebyshev_weights[0] * spectrum).reshape(shape)

    def mode_copies(level):
        return (
            remote(
                modes.at[level], beside.at[level, 0], mode_send.at[level, 0], mode_recv.at[level, 0], plane_next
            ),
            remote(
                modes.at[level], beside.at[level, 1], mode_send.at[level, 1], mode_recv.at[level, 1], plane_before
            ),
        )

    plane_low, plane_high = 4.0 * low(plane_cell), 4.0 * high(plane_cell)
    for level in range(POISSON - 1):
        for copy in mode_copies(level):
            copy.start()
        for copy in mode_copies(level):
            copy.wait()
        weight = chebyshev_weights[level + 1]

        def smooth(index, level=level, weight=weight):
            block = modes[level, index]
            around = plane_low * beside[level, 0, index] + plane_high * beside[level, 1, index]
            around = around + normal_before(block) + normal_after(block)
            scale = scale_ref[pl.ds(pl.multiple_of(index * span_cells, span_cells), span_cells), :]
            modes[level + 1, index] = (1.0 - weight) * block + weight * (rhs[index] + scale * around)

        loop(0, count_z, smooth)
    whole = modes[POISSON - 1].reshape(span_total, normal_cells)
    back = jnp.dot(table_ref[...], whole, precision=highest, preferred_element_type=jnp.float32)
    rhs[...] = back.reshape(shape)

    def scatter_copy(offset):
        device = partner(0, offset)
        return remote(
            rhs.at[device[1]],
            pressure.at[plane_cell, plane_column],
            turn_send.at[1, offset],
            turn_recv.at[1, offset],
            device,
        )

    loop(1, count_z, lambda offset: scatter_copy(offset).start())
    pressure[plane_cell, plane_column] = rhs[gz]
    loop(1, count_z, lambda offset: scatter_copy(offset).wait())

    def first_row(index):
        cell, column = lax.div(index, columns), lax.rem(index, columns)
        pressure_row[index] = pressure[cell, column][:1]

    loop(0, cells, first_row)
    copies = (
        remote(pressure.at[0], pressure.at[stream_cells], mode_send.at[POISSON - 1, 0], mode_recv.at[POISSON - 1, 0], before_gx),
        remote(pressure_row, pressure_halo, mode_send.at[POISSON - 1, 1], mode_recv.at[POISSON - 1, 1], before_gz),
    )
    for copy in copies:
        copy.start()
    for copy in copies:
        copy.wait()

    pairs = [(i, j) for i in range(columns) for j in range(i, columns)]
    half = normal_cells // 2

    def finish(cell, sums):
        updated = []
        for column in range(columns):
            block = pressure[cell, column]
            gradient = (
                2.0 * (pressure[cell + 1, column] * high(cell) - block),
                normal_after(block) - block,
                span_after(block, pressure_halo[cell * columns + column]) - block,
            )
            updated.append([])
            for part in range(components):
                value = fields[SWEEPS, part, cell + 1, column] - gradient[part]
                solved_ref[part, cell, column] = value
                updated[column].append(factor_ref[part, cell, column] + 2.0 * shift * value)
        totals = []
        for total, (i, j) in zip(sums, pairs):
            product = updated[i][0] * updated[j][0]
            for part in range(1, components):
                product = product + updated[i][part] * updated[j][part]
            product = product[:, :half] + product[:, half:]
            totals.append(total + product[:8] + product[8:])
        return tuple(totals)

    zero = jnp.zeros((8, half), jnp.float32)
    sums = lax.fori_loop(0, stream_cells, finish, (zero,) * len(pairs))
    tile_rows = lax.broadcasted_iota(jnp.int32, (8, 128), 0)
    tile_lanes = lax.broadcasted_iota(jnp.int32, (8, 128), 1)
    tile = jnp.zeros((8, 128), jnp.float32)

    def put(tile, row, lane, value):
        return jnp.where((tile_rows == row) & (tile_lanes == lane), value, tile)

    for total, (i, j) in zip(sums, pairs):
        value = jnp.sum(jnp.sum(total, axis=1, keepdims=True), axis=0, keepdims=True)
        tile = put(tile, i, j, value)
        if i != j:
            tile = put(tile, j, i, value)
    line_lanes = lax.broadcasted_iota(jnp.int32, (1, normal_cells), 1)
    for sensor in range(cells_ref.shape[0]):
        part = jnp.clip(cells_ref[sensor, 0], 0, components - 1)
        span = cells_ref[sensor, 1] - gz * span_cells
        stream = cells_ref[sensor, 2] - gx * stream_cells
        inside = (span >= 0) & (span < span_cells) & (stream >= 0) & (stream < stream_cells)
        span = jnp.clip(span, 0, span_cells - 1)
        stream = jnp.clip(stream, 0, stream_cells - 1)
        chosen = (line_lanes == cells_ref[sensor, 3]) & inside
        for column in range(columns):
            line = solved_ref[part, stream, column, pl.ds(span, 1), :]
            value = jnp.sum(jnp.where(chosen, line, 0.0), axis=1, keepdims=True)
            tile = put(tile, columns + sensor, column, value)
    mid[0] = tile
    places = (gz, here_x, here_y)
    bases = (0, count_z, count_z + count_x)
    for stage, slots in enumerate((slots_z, slots_x, slots_y)):
        def sum_copy(offset, stage=stage, slots=slots):
            index = bases[stage] + offset
            return remote(
                mid.at[stage], slots.at[places[stage]], sum_send.at[index], sum_recv.at[index], partner(stage, offset)
            )

        loop(1, counts[stage], lambda offset, sum_copy=sum_copy: sum_copy(offset).start())
        slots[places[stage]] = mid[stage]
        loop(1, counts[stage], lambda offset, sum_copy=sum_copy: sum_copy(offset).wait())
        total = slots[0]
        for place in range(1, counts[stage]):
            total = total + slots[place]
        if stage < 2:
            mid[stage + 1] = total
        else:
            out_ref[...] = total


def hartley_table(span_total):
    index = np.arange(span_total)
    angles = 2.0 * math.pi * (index[:, None] * index[None, :] % span_total) / span_total
    return ((np.cos(angles) + np.sin(angles)) / math.sqrt(span_total)).astype(np.float32)


def mode_scale(span_total, normal_cells):
    wavenumber = 2.0 * math.pi * np.arange(span_total) / span_total
    diagonal = 10.0 + (2.0 - 2.0 * np.cos(wavenumber))
    return np.repeat((1.0 / diagonal).astype(np.float32)[:, None], normal_cells, axis=1)


def solve(shift, sensor_cells, turned_factor, turned_base, sizes):
    count_z, count_x, count_y = sizes
    components, stream_cells, columns, span_cells, normal_cells = turned_factor.shape
    cells = stream_cells * columns
    span_total = count_z * span_cells
    vmem = pl.BlockSpec(memory_space=pltpu.VMEM)
    smem = pl.BlockSpec(memory_space=pltpu.SMEM)
    f32 = jnp.float32
    group = (count_z, span_cells, normal_cells)
    dma = pltpu.SemaphoreType.DMA
    return pl.pallas_call(
        functools.partial(step_kernel, sizes),
        out_shape=(
            jax.ShapeDtypeStruct(turned_factor.shape, f32),
            jax.ShapeDtypeStruct((8, 128), f32),
        ),
        in_specs=[smem, smem, vmem, vmem, vmem, vmem],
        out_specs=(vmem, vmem),
        scratch_shapes=[
            pltpu.VMEM((SWEEPS + 1, components, stream_cells + 2, columns, span_cells, normal_cells), f32),
            pltpu.VMEM((stream_cells, span_cells, normal_cells), f32),
            pltpu.VMEM((SWEEPS + 1, components, 2, cells, 1, normal_cells), f32),
            pltpu.VMEM((SWEEPS + 1, components, 2, cells, 1, normal_cells), f32),
            pltpu.VMEM(group, f32),
            pltpu.VMEM(group, f32),
            pltpu.VMEM(group, f32),
            pltpu.VMEM((POISSON,) + group, f32),
            pltpu.VMEM((POISSON - 1, 2) + group, f32),
            pltpu.VMEM((stream_cells + 1, columns, span_cells, normal_cells), f32),
            pltpu.VMEM((cells, 1, normal_cells), f32),
            pltpu.VMEM((cells, 1, normal_cells), f32),
        ]
        + [pltpu.VMEM((size, 8, 128), f32) for size in sizes]
        + [
            pltpu.VMEM((3, 8, 128), f32),
            dma((SWEEPS + 1, components, 4)),
            dma((SWEEPS + 1, components, 4)),
            dma((2, count_z)),
            dma((2, count_z)),
            dma((POISSON, 2)),
            dma((POISSON, 2)),
            dma((sum(sizes),)),
            dma((sum(sizes),)),
        ],
        compiler_params=pltpu.CompilerParams(collective_id=0, has_side_effects=True),
        name="solve",
    )(
        shift,
        sensor_cells,
        turned_factor,
        turned_base,
        jnp.asarray(hartley_table(span_total)),
        jnp.asarray(mode_scale(span_total, normal_cells)),
    )


def shards(factor, gain, base_flow, shift_index, sensor_cells):
    components, span_cells, columns, stream_cells, normal_cells = factor.shape
    count_gx, count_z = lax.axis_size("gx"), lax.axis_size("gz")
    count_x = 4 if count_gx % 4 == 0 else count_gx
    sizes = (count_z, count_x, count_gx // count_x)
    shift_values = jnp.asarray(shift_table, jnp.float32)
    shift_value = jnp.sum(jnp.where(jnp.arange(SHIFTS) == shift_index[0], shift_values, 0.0))
    solved, tile = solve(
        shift_value[None],
        sensor_cells,
        jnp.transpose(factor, (0, 3, 2, 1, 4)),
        jnp.transpose(base_flow, (1, 0, 2)),
        sizes,
    )
    solved = jnp.transpose(solved, (0, 3, 2, 1, 4))
    gram_total, readout = tile[:columns, :columns], tile[columns : 2 * columns, :columns]
    new_factor = factor + 2.0 * shift_value * solved
    total_cells = components * stream_cells * count_gx * normal_cells * span_cells * count_z
    gram = gram_total / float(total_cells)
    added = solved[:, :, 0:1] * readout[None, None, :, 0, None, None]
    for column in range(1, columns):
        added = added + solved[:, :, column : column + 1] * readout[None, None, :, column, None, None]
    new_gain = gain + 2.0 * shift_value * added
    return (new_factor, new_gain, gram)


def solution(mesh):
    placed = (
        P(None, "gz", None, "gx", None),
        P(None, "gz", None, "gx", None),
        P("gz", "gx", None),
        P(),
        P(),
    )
    return jax.shard_map(
        shards,
        mesh=mesh,
        in_specs=placed,
        out_specs=(P(None, "gz", None, "gx", None), P(None, "gz", None, "gx", None), P()),
        check_vma=False,
    )
```

```python
import functools
import math

import jax
import jax.numpy as jnp
import numpy as np
from jax import lax
from jax.experimental import pallas as pl
from jax.experimental.pallas import tpu as pltpu
from jax.sharding import PartitionSpec as P

SWEEPS = 3
POISSON = 4
SHIFTS = 8


viscosity = 0.4
shift_table = (0.6, 0.8, 1.0, 1.25, 1.6, 2.0, 2.5, 3.2)
chebyshev_weights = (1.0 / 1.9352976, 1.0 / 1.4752809, 1.0 / 0.8247191, 1.0 / 0.3647024)
highest = lax.Precision.HIGHEST


def step_kernel(
    sizes,
    shift_ref,
    cells_ref,
    factor_ref,
    base_ref,
    table_ref,
    scale_ref,
    solved_ref,
    out_ref,
    fields,
    inverse,
    row_sends,
    row_halos,
    blocks,
    planes,
    rhs,
    modes,
    beside,
    pressure,
    pressure_row,
    pressure_halo,
    slots_z,
    slots_x,
    slots_y,
    mid,
    halo_send,
    halo_recv,
    turn_send,
    turn_recv,
    mode_send,
    mode_recv,
    sum_send,
    sum_recv,
):
    count_z, count_x, count_y = sizes
    count_gx = count_x * count_y
    components, stream_cells, columns, span_cells, normal_cells = factor_ref.shape
    last_cell = stream_cells - 1
    cells = stream_cells * columns
    gx, gz = lax.axis_index("gx"), lax.axis_index("gz")
    here_x, here_y = gx % count_x, gx // count_x
    next_gx = ((gx + 1) % count_gx, gz)
    before_gx = ((gx + count_gx - 1) % count_gx, gz)
    next_gz = (gx, (gz + 1) % count_z)
    before_gz = (gx, (gz + count_z - 1) % count_z)
    shift = jnp.float32(shift_table[0])
    for entry in range(1, SHIFTS):
        shift = jnp.where(shift_ref[0] == entry, jnp.float32(shift_table[entry]), shift)

    odd = gx % 2
    turn = 1 - 2 * odd

    def mirrored(cell):
        return odd * last_cell + turn * cell

    plane_cell = mirrored(gz % stream_cells)
    plane_column = gz // stream_cells
    at_end = plane_cell // last_cell
    at_start = (last_cell - plane_cell) // last_cell
    plane_next = ((gx + at_end) % count_gx, gz + turn * (1 - at_end))
    plane_before = ((gx + count_gx - at_start) % count_gx, gz - turn * (1 - at_start))

    def low(cell):
        return jnp.where(gx + cell == 0, 0.0, 1.0)

    def high(cell):
        return jnp.where(count_gx - 1 - gx + last_cell - cell == 0, 0.0, 1.0)

    def partner(stage, offset):
        if stage == 0:
            return (gx, (gz + offset) % count_z)
        if stage == 1:
            return (here_y * count_x + (here_x + offset) % count_x, gz)
        return ((here_y + offset) % count_y * count_x + here_x, gz)

    def remote(src, dst, send, recv, device):
        return pltpu.make_async_remote_copy(
            src_ref=src,
            dst_ref=dst,
            send_sem=send,
            recv_sem=recv,
            device_id=device,
            device_id_type=pl.DeviceIdType.MESH,
        )

    def loop(first, end, act):
        def run(index, carry):
            act(index)
            return carry

        lax.fori_loop(first, end, run, 0)

    counts = (count_z, count_x, count_y)
    barrier = pltpu.get_barrier_semaphore()

    def greet(device):
        pl.semaphore_signal(barrier, inc=1, device_id=device, device_id_type=pl.DeviceIdType.MESH)

    for stage in range(3):
        loop(1, counts[stage], lambda offset, stage=stage: greet(partner(stage, offset)))
    greet(next_gx)
    greet(before_gx)

    rows = lax.broadcasted_iota(jnp.int32, (span_cells, normal_cells), 0)
    lanes = lax.broadcasted_iota(jnp.int32, (span_cells, normal_cells), 1)

    def normal_before(block):
        return jnp.where(lanes == 0, 0.0, pltpu.roll(block, 1, 1))

    def normal_after(block):
        return jnp.where(lanes == normal_cells - 1, 0.0, pltpu.roll(block, normal_cells - 1, 1))

    def span_before(block, halo):
        return jnp.where(rows == 0, halo, pltpu.roll(block, 1, 0))

    def span_after(block, halo):
        return jnp.where(rows == span_cells - 1, halo, pltpu.roll(block, span_cells - 1, 0))

    def halo_copies(level, part):
        moves = (
            (fields.at[level, part, stream_cells], fields.at[level, part, 0], next_gx),
            (fields.at[level, part, 1], fields.at[level, part, stream_cells + 1], before_gx),
            (row_sends.at[level, part, 0], row_halos.at[level, part, 0], next_gz),
            (row_sends.at[level, part, 1], row_halos.at[level, part, 1], before_gz),
        )
        sides = (0, 1, 2, 3) if level < SWEEPS else ((0,), (), (2,))[part]
        copies = []
        for side in sides:
            src, dst, device = moves[side]
            copies.append(
                remote(src, dst, halo_send.at[level, part, side], halo_recv.at[level, part, side], device)
            )
        return copies

    def keep(level, part, cell, column, block):
        index = cell * columns + column
        fields[level, part, cell + 1, column] = block
        row_sends[level, part, 0, index] = block[span_cells - 1 :]
        row_sends[level, part, 1, index] = block[:1]

    def invert(cell):
        inverse[cell] = 1.0 / (shift + 6.0 * viscosity + base_ref[cell])

    loop(0, stream_cells, invert)
    for part in range(components):
        def first_guess(cell, part=part):
            for column in range(columns):
                keep(0, part, cell, column, -factor_ref[part, cell, column] * inverse[cell])

        loop(0, stream_cells, first_guess)
        if part == 0:
            pl.semaphore_wait(barrier, sum(counts) - 3 + 2)
        for copy in halo_copies(0, part):
            copy.start()
    for level in range(SWEEPS):
        for part in range(components):
            for copy in halo_copies(level, part):
                copy.wait()

            def sweep(cell, level=level, part=part):
                for column in range(columns):
                    index = cell * columns + column
                    block = fields[level, part, cell + 1, column]
                    behind = fields[level, part, cell, column] * low(cell)
                    around = behind + fields[level, part, cell + 2, column] * high(cell)
                    around = around + normal_before(block) + normal_after(block)
                    around = around + span_before(block, row_halos[level, part, 0, index])
                    around = around + span_after(block, row_halos[level, part, 1, index])
                    total = viscosity * around + base_ref[cell] * behind
                    total = total - factor_ref[part, cell, column]
                    keep(level + 1, part, cell, column, total * inverse[cell])

            loop(0, stream_cells, sweep)
            for copy in halo_copies(level + 1, part):
                copy.start()
    for part in range(components):
        for copy in halo_copies(SWEEPS, part):
            copy.wait()

    def spread(step):
        return count_z // 2 + step // 2 * (1 - 2 * (step % 2))

    def diverge(target):
        cell, column = mirrored(target % stream_cells), target // stream_cells
        index = cell * columns + column
        normal = fields[SWEEPS, 1, cell + 1, column]
        span = fields[SWEEPS, 2, cell + 1, column]
        total = 2.0 * (
            fields[SWEEPS, 0, cell + 1, column] - fields[SWEEPS, 0, cell, column] * low(cell)
        )
        total = total + (normal - normal_before(normal))
        return -(total + (span - span_before(span, row_halos[SWEEPS, 2, 0, index])))

    def gather_copy(step):
        offset = spread(step)
        device = partner(0, offset)
        return remote(
            blocks.at[device[1]], planes.at[gz], turn_send.at[0, offset], turn_recv.at[0, offset], device
        )

    def gather_start(step):
        target = partner(0, spread(step))[1]
        blocks[target] = diverge(target)
        gather_copy(step).start()

    loop(1, count_z, gather_start)
    planes[gz] = diverge(gz)
    loop(1, count_z, lambda step: gather_copy(step).wait())
    span_total = count_z * span_cells
    chunks = 4
    group = count_z // chunks
    height = span_total // chunks
    shape = (group, span_cells, normal_cells)

    def mode_copies(level, chunk):
        part = pl.ds(chunk * group, group)
        return [
            remote(
                modes.at[level, part],
                beside.at[level, side, part],
                mode_send.at[level, side, chunk],
                mode_recv.at[level, side, chunk],
                device,
            )
            for side, device in enumerate((plane_next, plane_before))
        ]

    whole = planes[...].reshape(span_total, normal_cells)
    for chunk in range(chunks):
        lines = slice(chunk * height, (chunk + 1) * height)
        spectrum = jnp.dot(
            table_ref[lines, :], whole, precision=highest, preferred_element_type=jnp.float32
        ) * scale_ref[lines, :]
        part = slice(chunk * group, (chunk + 1) * group)
        rhs[part] = spectrum.reshape(shape)
        modes[0, part] = (chebyshev_weights[0] * spectrum).reshape(shape)
        for copy in mode_copies(0, chunk):
            copy.start()

    plane_low, plane_high = 4.0 * low(plane_cell), 4.0 * high(plane_cell)
    for level in range(POISSON - 1):
        weight = chebyshev_weights[level + 1]
        for chunk in range(chunks):
            for copy in mode_copies(level, chunk):
                copy.wait()
            for index in range(chunk * group, (chunk + 1) * group):
                block = modes[level, index]
                around = plane_low * beside[level, 0, index] + plane_high * beside[level, 1, index]
                around = around + normal_before(block) + normal_after(block)
                scale = scale_ref[index * span_cells : (index + 1) * span_cells, :]
                modes[level + 1, index] = (1.0 - weight) * block + weight * (rhs[index] + scale * around)
            if level < POISSON - 2:
                for copy in mode_copies(level + 1, chunk):
                    copy.start()
    whole = modes[POISSON - 1].reshape(span_total, normal_cells)
    back = jnp.dot(table_ref[...], whole, precision=highest, preferred_element_type=jnp.float32)
    blocks[...] = back.reshape(count_z, span_cells, normal_cells)

    def scatter_copy(step):
        offset = spread(step)
        device = partner(0, offset)
        return remote(
            blocks.at[device[1]],
            pressure.at[plane_cell, plane_column],
            turn_send.at[1, offset],
            turn_recv.at[1, offset],
            device,
        )

    loop(1, count_z, lambda step: scatter_copy(step).start())
    pressure[plane_cell, plane_column] = blocks[gz]
    loop(1, count_z, lambda step: scatter_copy(step).wait())

    for cell in range(stream_cells):
        for column in range(columns):
            pressure_row[cell * columns + column] = pressure[cell, column][:1]
    copies = (
        remote(pressure.at[0], pressure.at[stream_cells], mode_send.at[POISSON - 1, 0, 0], mode_recv.at[POISSON - 1, 0, 0], before_gx),
        remote(pressure_row, pressure_halo, mode_send.at[POISSON - 1, 1, 0], mode_recv.at[POISSON - 1, 1, 0], before_gz),
    )
    for copy in copies:
        copy.start()
    for copy in copies:
        copy.wait()

    pairs = [(i, j) for i in range(columns) for j in range(i, columns)]
    half = normal_cells // 2

    def finish(cell, sums):
        updated = []
        for column in range(columns):
            block = pressure[cell, column]
            gradient = (
                2.0 * (pressure[cell + 1, column] * high(cell) - block),
                normal_after(block) - block,
                span_after(block, pressure_halo[cell * columns + column]) - block,
            )
            updated.append([])
            for part in range(components):
                value = fields[SWEEPS, part, cell + 1, column] - gradient[part]
                solved_ref[part, cell, column] = value
                updated[column].append(factor_ref[part, cell, column] + 2.0 * shift * value)
        totals = []
        for total, (i, j) in zip(sums, pairs):
            product = updated[i][0] * updated[j][0]
            for part in range(1, components):
                product = product + updated[i][part] * updated[j][part]
            product = product[:, :half] + product[:, half:]
            totals.append(total + product[:8] + product[8:])
        return tuple(totals)

    zero = jnp.zeros((8, half), jnp.float32)
    sums = lax.fori_loop(0, stream_cells, finish, (zero,) * len(pairs))
    tile_rows = lax.broadcasted_iota(jnp.int32, (8, 128), 0)
    tile_lanes = lax.broadcasted_iota(jnp.int32, (8, 128), 1)
    tile = jnp.zeros((8, 128), jnp.float32)

    def put(tile, row, lane, value):
        return jnp.where((tile_rows == row) & (tile_lanes == lane), value, tile)

    for total, (i, j) in zip(sums, pairs):
        value = jnp.sum(jnp.sum(total, axis=1, keepdims=True), axis=0, keepdims=True)
        tile = put(tile, i, j, value)
        if i != j:
            tile = put(tile, j, i, value)
    line_lanes = lax.broadcasted_iota(jnp.int32, (1, normal_cells), 1)
    for sensor in range(cells_ref.shape[0]):
        part = jnp.clip(cells_ref[sensor, 0], 0, components - 1)
        span = cells_ref[sensor, 1] - gz * span_cells
        stream = cells_ref[sensor, 2] - gx * stream_cells
        inside = (span >= 0) & (span < span_cells) & (stream >= 0) & (stream < stream_cells)
        span = jnp.clip(span, 0, span_cells - 1)
        stream = jnp.clip(stream, 0, stream_cells - 1)
        chosen = (line_lanes == cells_ref[sensor, 3]) & inside
        for column in range(columns):
            line = solved_ref[part, stream, column, pl.ds(span, 1), :]
            value = jnp.sum(jnp.where(chosen, line, 0.0), axis=1, keepdims=True)
            tile = put(tile, columns + sensor, column, value)
    mid[0] = tile
    places = (gz, here_x, here_y)
    bases = (0, count_z, count_z + count_x)
    for stage, slots in enumerate((slots_z, slots_x, slots_y)):
        def sum_copy(offset, stage=stage, slots=slots):
            index = bases[stage] + offset
            return remote(
                mid.at[stage], slots.at[places[stage]], sum_send.at[index], sum_recv.at[index], partner(stage, offset)
            )

        loop(1, counts[stage], lambda offset, sum_copy=sum_copy: sum_copy(offset).start())
        slots[places[stage]] = mid[stage]
        loop(1, counts[stage], lambda offset, sum_copy=sum_copy: sum_copy(offset).wait())
        total = slots[0]
        for place in range(1, counts[stage]):
            total = total + slots[place]
        if stage < 2:
            mid[stage + 1] = total
        else:
            out_ref[...] = total


def hartley_table(span_total):
    index = np.arange(span_total)
    angles = 2.0 * math.pi * (index[:, None] * index[None, :] % span_total) / span_total
    return ((np.cos(angles) + np.sin(angles)) / math.sqrt(span_total)).astype(np.float32)


def mode_scale(span_total, normal_cells):
    wavenumber = 2.0 * math.pi * np.arange(span_total) / span_total
    diagonal = 10.0 + (2.0 - 2.0 * np.cos(wavenumber))
    return np.repeat((1.0 / diagonal).astype(np.float32)[:, None], normal_cells, axis=1)


def solve(shift, sensor_cells, turned_factor, turned_base, sizes):
    count_z, count_x, count_y = sizes
    components, stream_cells, columns, span_cells, normal_cells = turned_factor.shape
    cells = stream_cells * columns
    span_total = count_z * span_cells
    vmem = pl.BlockSpec(memory_space=pltpu.VMEM)
    smem = pl.BlockSpec(memory_space=pltpu.SMEM)
    f32 = jnp.float32
    group = (count_z, span_cells, normal_cells)
    dma = pltpu.SemaphoreType.DMA
    return pl.pallas_call(
        functools.partial(step_kernel, sizes),
        out_shape=(
            jax.ShapeDtypeStruct(turned_factor.shape, f32),
            jax.ShapeDtypeStruct((8, 128), f32),
        ),
        in_specs=[smem, smem, vmem, vmem, vmem, vmem],
        out_specs=(vmem, vmem),
        scratch_shapes=[
            pltpu.VMEM((SWEEPS + 1, components, stream_cells + 2, columns, span_cells, normal_cells), f32),
            pltpu.VMEM((stream_cells, span_cells, normal_cells), f32),
            pltpu.VMEM((SWEEPS + 1, components, 2, cells, 1, normal_cells), f32),
            pltpu.VMEM((SWEEPS + 1, components, 2, cells, 1, normal_cells), f32),
            pltpu.VMEM(group, f32),
            pltpu.VMEM(group, f32),
            pltpu.VMEM(group, f32),
            pltpu.VMEM((POISSON,) + group, f32),
            pltpu.VMEM((POISSON - 1, 2) + group, f32),
            pltpu.VMEM((stream_cells + 1, columns, span_cells, normal_cells), f32),
            pltpu.VMEM((cells, 1, normal_cells), f32),
            pltpu.VMEM((cells, 1, normal_cells), f32),
        ]
        + [pltpu.VMEM((size, 8, 128), f32) for size in sizes]
        + [
            pltpu.VMEM((3, 8, 128), f32),
            dma((SWEEPS + 1, components, 4)),
            dma((SWEEPS + 1, components, 4)),
            dma((2, count_z)),
            dma((2, count_z)),
            dma((POISSON, 2, 4)),
            dma((POISSON, 2, 4)),
            dma((sum(sizes),)),
            dma((sum(sizes),)),
        ],
        compiler_params=pltpu.CompilerParams(collective_id=0, has_side_effects=True),
        name="solve",
    )(
        shift,
        sensor_cells,
        turned_factor,
        turned_base,
        jnp.asarray(hartley_table(span_total)),
        jnp.asarray(mode_scale(span_total, normal_cells)),
    )


def shards(factor, gain, base_flow, shift_index, sensor_cells):
    components, span_cells, columns, stream_cells, normal_cells = factor.shape
    count_gx, count_z = lax.axis_size("gx"), lax.axis_size("gz")
    count_x = 4 if count_gx % 4 == 0 else count_gx
    sizes = (count_z, count_x, count_gx // count_x)
    shift_values = jnp.asarray(shift_table, jnp.float32)
    shift_value = jnp.sum(jnp.where(jnp.arange(SHIFTS) == shift_index[0], shift_values, 0.0))
    solved, tile = solve(
        shift_index,
        sensor_cells,
        jnp.transpose(factor, (0, 3, 2, 1, 4)),
        jnp.transpose(base_flow, (1, 0, 2)),
        sizes,
    )
    solved = jnp.transpose(solved, (0, 3, 2, 1, 4))
    gram_total, readout = tile[:columns, :columns], tile[columns : 2 * columns, :columns]
    new_factor = factor + 2.0 * shift_value * solved
    total_cells = components * stream_cells * count_gx * normal_cells * span_cells * count_z
    gram = gram_total / float(total_cells)
    added = solved[:, :, 0:1] * readout[None, None, :, 0, None, None]
    for column in range(1, columns):
        added = added + solved[:, :, column : column + 1] * readout[None, None, :, column, None, None]
    new_gain = gain + 2.0 * shift_value * added
    return (new_factor, new_gain, gram)


def solution(mesh):
    placed = (
        P(None, "gz", None, "gx", None),
        P(None, "gz", None, "gx", None),
        P("gz", "gx", None),
        P(),
        P(),
    )
    return jax.shard_map(
        shards,
        mesh=mesh,
        in_specs=placed,
        out_specs=(P(None, "gz", None, "gx", None), P(None, "gz", None, "gx", None), P()),
        check_vma=False,
    )
```

```python
import functools
import math

import jax
import jax.numpy as jnp
import numpy as np
from jax import lax
from jax.experimental import pallas as pl
from jax.experimental.pallas import tpu as pltpu
from jax.sharding import PartitionSpec as P

SWEEPS = 3
POISSON = 4
SHIFTS = 8


viscosity = 0.4
shift_table = (0.6, 0.8, 1.0, 1.25, 1.6, 2.0, 2.5, 3.2)
chebyshev_weights = (1.0 / 1.9352976, 1.0 / 1.4752809, 1.0 / 0.8247191, 1.0 / 0.3647024)
highest = lax.Precision.HIGHEST


def step_kernel(
    sizes,
    shift_ref,
    cells_ref,
    given_factor,
    gain_ref,
    given_base,
    table_ref,
    scale_ref,
    new_factor_ref,
    new_gain_ref,
    gram_ref,
    factor_ref,
    base_ref,
    solved_ref,
    natural,
    fields,
    inverse,
    row_sends,
    row_halos,
    blocks,
    planes,
    rhs,
    modes,
    beside,
    pressure,
    pressure_row,
    pressure_halo,
    slots_z,
    slots_x,
    slots_y,
    mid,
    halo_send,
    halo_recv,
    turn_send,
    turn_recv,
    mode_send,
    mode_recv,
    sum_send,
    sum_recv,
):
    count_z, count_x, count_y = sizes
    count_gx = count_x * count_y
    components, span_cells, columns, stream_cells, normal_cells = given_factor.shape
    last_cell = stream_cells - 1
    cells = stream_cells * columns
    gx, gz = lax.axis_index("gx"), lax.axis_index("gz")
    here_x, here_y = gx % count_x, gx // count_x
    next_gx = ((gx + 1) % count_gx, gz)
    before_gx = ((gx + count_gx - 1) % count_gx, gz)
    next_gz = (gx, (gz + 1) % count_z)
    before_gz = (gx, (gz + count_z - 1) % count_z)
    shift = jnp.float32(shift_table[0])
    for entry in range(1, SHIFTS):
        shift = jnp.where(shift_ref[0] == entry, jnp.float32(shift_table[entry]), shift)

    odd = gx % 2
    turn = 1 - 2 * odd

    def mirrored(cell):
        return odd * last_cell + turn * cell

    plane_cell = mirrored(gz % stream_cells)
    plane_column = gz // stream_cells
    at_end = plane_cell // last_cell
    at_start = (last_cell - plane_cell) // last_cell
    plane_next = ((gx + at_end) % count_gx, gz + turn * (1 - at_end))
    plane_before = ((gx + count_gx - at_start) % count_gx, gz - turn * (1 - at_start))

    def low(cell):
        return jnp.where(gx + cell == 0, 0.0, 1.0)

    def high(cell):
        return jnp.where(count_gx - 1 - gx + last_cell - cell == 0, 0.0, 1.0)

    def partner(stage, offset):
        if stage == 0:
            return (gx, (gz + offset) % count_z)
        if stage == 1:
            return (here_y * count_x + (here_x + offset) % count_x, gz)
        return ((here_y + offset) % count_y * count_x + here_x, gz)

    def remote(src, dst, send, recv, device):
        return pltpu.make_async_remote_copy(
            src_ref=src,
            dst_ref=dst,
            send_sem=send,
            recv_sem=recv,
            device_id=device,
            device_id_type=pl.DeviceIdType.MESH,
        )

    def loop(first, end, act):
        def run(index, carry):
            act(index)
            return carry

        lax.fori_loop(first, end, run, 0)

    counts = (count_z, count_x, count_y)
    barrier = pltpu.get_barrier_semaphore()

    def greet(device):
        pl.semaphore_signal(barrier, inc=1, device_id=device, device_id_type=pl.DeviceIdType.MESH)

    for stage in range(3):
        loop(1, counts[stage], lambda offset, stage=stage: greet(partner(stage, offset)))
    greet(next_gx)
    greet(before_gx)

    rows = lax.broadcasted_iota(jnp.int32, (span_cells, normal_cells), 0)
    lanes = lax.broadcasted_iota(jnp.int32, (span_cells, normal_cells), 1)

    def normal_before(block):
        return jnp.where(lanes == 0, 0.0, pltpu.roll(block, 1, 1))

    def normal_after(block):
        return jnp.where(lanes == normal_cells - 1, 0.0, pltpu.roll(block, normal_cells - 1, 1))

    def span_before(block, halo):
        return jnp.where(rows == 0, halo, pltpu.roll(block, 1, 0))

    def span_after(block, halo):
        return jnp.where(rows == span_cells - 1, halo, pltpu.roll(block, span_cells - 1, 0))

    def halo_copies(level, part):
        moves = (
            (fields.at[level, part, stream_cells], fields.at[level, part, 0], next_gx),
            (fields.at[level, part, 1], fields.at[level, part, stream_cells + 1], before_gx),
            (row_sends.at[level, part, 0], row_halos.at[level, part, 0], next_gz),
            (row_sends.at[level, part, 1], row_halos.at[level, part, 1], before_gz),
        )
        sides = (0, 1, 2, 3) if level < SWEEPS else ((0,), (), (2,))[part]
        copies = []
        for side in sides:
            src, dst, device = moves[side]
            copies.append(
                remote(src, dst, halo_send.at[level, part, side], halo_recv.at[level, part, side], device)
            )
        return copies

    def keep(level, part, cell, column, block):
        index = cell * columns + column
        fields[level, part, cell + 1, column] = block
        row_sends[level, part, 0, index] = block[span_cells - 1 :]
        row_sends[level, part, 1, index] = block[:1]

    for cell in range(stream_cells):
        base_ref[cell] = given_base[:, cell, :]
        inverse[cell] = 1.0 / (shift + 6.0 * viscosity + base_ref[cell])
    for part in range(components):
        for cell in range(stream_cells):
            for column in range(columns):
                block = given_factor[part, :, column, cell, :]
                factor_ref[part, cell, column] = block
                keep(0, part, cell, column, -block * inverse[cell])
        if part == 0:
            pl.semaphore_wait(barrier, sum(counts) - 3 + 2)
        for copy in halo_copies(0, part):
            copy.start()
    for level in range(SWEEPS):
        for part in range(components):
            for copy in halo_copies(level, part):
                copy.wait()

            def sweep(cell, level=level, part=part):
                for column in range(columns):
                    index = cell * columns + column
                    block = fields[level, part, cell + 1, column]
                    behind = fields[level, part, cell, column] * low(cell)
                    around = behind + fields[level, part, cell + 2, column] * high(cell)
                    around = around + normal_before(block) + normal_after(block)
                    around = around + span_before(block, row_halos[level, part, 0, index])
                    around = around + span_after(block, row_halos[level, part, 1, index])
                    total = viscosity * around + base_ref[cell] * behind
                    total = total - factor_ref[part, cell, column]
                    keep(level + 1, part, cell, column, total * inverse[cell])

            loop(0, stream_cells, sweep)
            for copy in halo_copies(level + 1, part):
                copy.start()
    for part in range(components):
        for copy in halo_copies(SWEEPS, part):
            copy.wait()

    def spread(step):
        return count_z // 2 + step // 2 * (1 - 2 * (step % 2))

    def diverge(target):
        cell, column = mirrored(target % stream_cells), target // stream_cells
        index = cell * columns + column
        normal = fields[SWEEPS, 1, cell + 1, column]
        span = fields[SWEEPS, 2, cell + 1, column]
        total = 2.0 * (
            fields[SWEEPS, 0, cell + 1, column] - fields[SWEEPS, 0, cell, column] * low(cell)
        )
        total = total + (normal - normal_before(normal))
        return -(total + (span - span_before(span, row_halos[SWEEPS, 2, 0, index])))

    def gather_copy(step):
        offset = spread(step)
        device = partner(0, offset)
        return remote(
            blocks.at[device[1]], planes.at[gz], turn_send.at[0, offset], turn_recv.at[0, offset], device
        )

    def gather_start(step):
        target = partner(0, spread(step))[1]
        blocks[target] = diverge(target)
        gather_copy(step).start()

    loop(1, count_z, gather_start)
    planes[gz] = diverge(gz)
    loop(1, count_z, lambda step: gather_copy(step).wait())
    span_total = count_z * span_cells
    chunks = 4
    group = count_z // chunks
    height = span_total // chunks
    shape = (group, span_cells, normal_cells)

    def mode_copies(level, chunk):
        part = pl.ds(chunk * group, group)
        return [
            remote(
                modes.at[level, part],
                beside.at[level, side, part],
                mode_send.at[level, side, chunk],
                mode_recv.at[level, side, chunk],
                device,
            )
            for side, device in enumerate((plane_next, plane_before))
        ]

    whole = planes[...].reshape(span_total, normal_cells)
    for chunk in range(chunks):
        lines = slice(chunk * height, (chunk + 1) * height)
        spectrum = jnp.dot(
            table_ref[lines, :], whole, precision=highest, preferred_element_type=jnp.float32
        ) * scale_ref[lines, :]
        part = slice(chunk * group, (chunk + 1) * group)
        rhs[part] = spectrum.reshape(shape)
        modes[0, part] = (chebyshev_weights[0] * spectrum).reshape(shape)
        for copy in mode_copies(0, chunk):
            copy.start()

    plane_low, plane_high = 4.0 * low(plane_cell), 4.0 * high(plane_cell)
    for level in range(POISSON - 1):
        weight = chebyshev_weights[level + 1]
        for chunk in range(chunks):
            for copy in mode_copies(level, chunk):
                copy.wait()
            for index in range(chunk * group, (chunk + 1) * group):
                block = modes[level, index]
                around = plane_low * beside[level, 0, index] + plane_high * beside[level, 1, index]
                around = around + normal_before(block) + normal_after(block)
                scale = scale_ref[index * span_cells : (index + 1) * span_cells, :]
                modes[level + 1, index] = (1.0 - weight) * block + weight * (rhs[index] + scale * around)
            if level < POISSON - 2:
                for copy in mode_copies(level + 1, chunk):
                    copy.start()
    whole = modes[POISSON - 1].reshape(span_total, normal_cells)
    back = jnp.dot(table_ref[...], whole, precision=highest, preferred_element_type=jnp.float32)
    blocks[...] = back.reshape(count_z, span_cells, normal_cells)

    def scatter_copy(step):
        offset = spread(step)
        device = partner(0, offset)
        return remote(
            blocks.at[device[1]],
            pressure.at[plane_cell, plane_column],
            turn_send.at[1, offset],
            turn_recv.at[1, offset],
            device,
        )

    loop(1, count_z, lambda step: scatter_copy(step).start())
    pressure[plane_cell, plane_column] = blocks[gz]
    loop(1, count_z, lambda step: scatter_copy(step).wait())

    for cell in range(stream_cells):
        for column in range(columns):
            pressure_row[cell * columns + column] = pressure[cell, column][:1]
    copies = (
        remote(pressure.at[0], pressure.at[stream_cells], mode_send.at[POISSON - 1, 0, 0], mode_recv.at[POISSON - 1, 0, 0], before_gx),
        remote(pressure_row, pressure_halo, mode_send.at[POISSON - 1, 1, 0], mode_recv.at[POISSON - 1, 1, 0], before_gz),
    )
    for copy in copies:
        copy.start()
    for copy in copies:
        copy.wait()

    pairs = [(i, j) for i in range(columns) for j in range(i, columns)]
    half = normal_cells // 2

    def finish(cell, sums):
        updated = []
        for column in range(columns):
            block = pressure[cell, column]
            gradient = (
                2.0 * (pressure[cell + 1, column] * high(cell) - block),
                normal_after(block) - block,
                span_after(block, pressure_halo[cell * columns + column]) - block,
            )
            updated.append([])
            for part in range(components):
                value = fields[SWEEPS, part, cell + 1, column] - gradient[part]
                solved_ref[part, cell, column] = value
                updated[column].append(factor_ref[part, cell, column] + 2.0 * shift * value)
        totals = []
        for total, (i, j) in zip(sums, pairs):
            product = updated[i][0] * updated[j][0]
            for part in range(1, components):
                product = product + updated[i][part] * updated[j][part]
            product = product[:, :half] + product[:, half:]
            totals.append(total + product[:8] + product[8:])
        return tuple(totals)

    zero = jnp.zeros((8, half), jnp.float32)
    sums = lax.fori_loop(0, stream_cells, finish, (zero,) * len(pairs))
    tile_rows = lax.broadcasted_iota(jnp.int32, (8, 128), 0)
    tile_lanes = lax.broadcasted_iota(jnp.int32, (8, 128), 1)
    tile = jnp.zeros((8, 128), jnp.float32)

    def put(tile, row, lane, value):
        return jnp.where((tile_rows == row) & (tile_lanes == lane), value, tile)

    for total, (i, j) in zip(sums, pairs):
        value = jnp.sum(jnp.sum(total, axis=1, keepdims=True), axis=0, keepdims=True)
        tile = put(tile, i, j, value)
        if i != j:
            tile = put(tile, j, i, value)
    line_lanes = lax.broadcasted_iota(jnp.int32, (1, normal_cells), 1)
    for sensor in range(cells_ref.shape[0]):
        part = jnp.clip(cells_ref[sensor, 0], 0, components - 1)
        span = cells_ref[sensor, 1] - gz * span_cells
        stream = cells_ref[sensor, 2] - gx * stream_cells
        inside = (span >= 0) & (span < span_cells) & (stream >= 0) & (stream < stream_cells)
        span = jnp.clip(span, 0, span_cells - 1)
        stream = jnp.clip(stream, 0, stream_cells - 1)
        chosen = (line_lanes == cells_ref[sensor, 3]) & inside
        for column in range(columns):
            line = solved_ref[part, stream, column, pl.ds(span, 1), :]
            value = jnp.sum(jnp.where(chosen, line, 0.0), axis=1, keepdims=True)
            tile = put(tile, columns + sensor, column, value)
    mid[0] = tile
    places = (gz, here_x, here_y)
    bases = (0, count_z, count_z + count_x)
    for stage, slots in enumerate((slots_z, slots_x, slots_y)):
        def sum_copy(offset, stage=stage, slots=slots):
            index = bases[stage] + offset
            return remote(
                mid.at[stage], slots.at[places[stage]], sum_send.at[index], sum_recv.at[index], partner(stage, offset)
            )

        loop(1, counts[stage], lambda offset, sum_copy=sum_copy: sum_copy(offset).start())
        if stage == 0:
            for part in range(components):
                for cell in range(stream_cells):
                    for column in range(columns):
                        block = solved_ref[part, cell, column] * (2.0 * shift)
                        natural[part, :, column, cell, :] = block
                        new_factor_ref[part, :, column, cell, :] = factor_ref[part, cell, column] + block
        slots[places[stage]] = mid[stage]
        loop(1, counts[stage], lambda offset, sum_copy=sum_copy: sum_copy(offset).wait())
        total = slots[0]
        for place in range(1, counts[stage]):
            total = total + slots[place]
        if stage < 2:
            mid[stage + 1] = total
        else:
            gram_ref[...] = total[:columns, :columns] * (1.0 / (components * cells * normal_cells * span_cells * count_z * count_gx / columns))
            readout = [
                [total[columns + i : columns + i + 1, j : j + 1] for j in range(columns)] for i in range(columns)
            ]

            def gain(span):
                for part in range(components):
                    steps = [natural[part, span, j] for j in range(columns)]
                    for i in range(columns):
                        value = gain_ref[part, span, i]
                        for j in range(columns):
                            value = value + steps[j] * readout[i][j]
                        new_gain_ref[part, span, i] = value

            loop(0, span_cells, gain)


def hartley_table(span_total):
    index = np.arange(span_total)
    angles = 2.0 * math.pi * (index[:, None] * index[None, :] % span_total) / span_total
    return ((np.cos(angles) + np.sin(angles)) / math.sqrt(span_total)).astype(np.float32)


def mode_scale(span_total, normal_cells):
    wavenumber = 2.0 * math.pi * np.arange(span_total) / span_total
    diagonal = 10.0 + (2.0 - 2.0 * np.cos(wavenumber))
    return np.repeat((1.0 / diagonal).astype(np.float32)[:, None], normal_cells, axis=1)


def solve(factor, gain, base_flow, shift_index, sensor_cells, sizes):
    count_z, count_x, count_y = sizes
    components, span_cells, columns, stream_cells, normal_cells = factor.shape
    cells = stream_cells * columns
    span_total = count_z * span_cells
    vmem = pl.BlockSpec(memory_space=pltpu.VMEM)
    smem = pl.BlockSpec(memory_space=pltpu.SMEM)
    f32 = jnp.float32
    group = (count_z, span_cells, normal_cells)
    turned = (components, stream_cells, columns, span_cells, normal_cells)
    dma = pltpu.SemaphoreType.DMA
    return pl.pallas_call(
        functools.partial(step_kernel, sizes),
        out_shape=(
            jax.ShapeDtypeStruct(factor.shape, f32),
            jax.ShapeDtypeStruct(gain.shape, f32),
            jax.ShapeDtypeStruct((columns, columns), f32),
        ),
        in_specs=[smem, smem, vmem, vmem, vmem, vmem, vmem],
        out_specs=(vmem, vmem, vmem),
        scratch_shapes=[
            pltpu.VMEM(turned, f32),
            pltpu.VMEM((stream_cells, span_cells, normal_cells), f32),
            pltpu.VMEM(turned, f32),
            pltpu.VMEM(factor.shape, f32),
            pltpu.VMEM((SWEEPS + 1, components, stream_cells + 2, columns, span_cells, normal_cells), f32),
            pltpu.VMEM((stream_cells, span_cells, normal_cells), f32),
            pltpu.VMEM((SWEEPS + 1, components, 2, cells, 1, normal_cells), f32),
            pltpu.VMEM((SWEEPS + 1, components, 2, cells, 1, normal_cells), f32),
            pltpu.VMEM(group, f32),
            pltpu.VMEM(group, f32),
            pltpu.VMEM(group, f32),
            pltpu.VMEM((POISSON,) + group, f32),
            pltpu.VMEM((POISSON - 1, 2) + group, f32),
            pltpu.VMEM((stream_cells + 1, columns, span_cells, normal_cells), f32),
            pltpu.VMEM((cells, 1, normal_cells), f32),
            pltpu.VMEM((cells, 1, normal_cells), f32),
        ]
        + [pltpu.VMEM((size, 8, 128), f32) for size in sizes]
        + [
            pltpu.VMEM((3, 8, 128), f32),
            dma((SWEEPS + 1, components, 4)),
            dma((SWEEPS + 1, components, 4)),
            dma((2, count_z)),
            dma((2, count_z)),
            dma((POISSON, 2, 4)),
            dma((POISSON, 2, 4)),
            dma((sum(sizes),)),
            dma((sum(sizes),)),
        ],
        compiler_params=pltpu.CompilerParams(collective_id=0, has_side_effects=True),
        name="solve",
    )(
        shift_index,
        sensor_cells,
        factor,
        gain,
        base_flow,
        jnp.asarray(hartley_table(span_total)),
        jnp.asarray(mode_scale(span_total, normal_cells)),
    )


def shards(factor, gain, base_flow, shift_index, sensor_cells):
    count_gx, count_z = lax.axis_size("gx"), lax.axis_size("gz")
    count_x = 4 if count_gx % 4 == 0 else count_gx
    sizes = (count_z, count_x, count_gx // count_x)
    return solve(factor, gain, base_flow, shift_index, sensor_cells, sizes)


def solution(mesh):
    placed = (
        P(None, "gz", None, "gx", None),
        P(None, "gz", None, "gx", None),
        P("gz", "gx", None),
        P(),
        P(),
    )
    return jax.shard_map(
        shards,
        mesh=mesh,
        in_specs=placed,
        out_specs=(P(None, "gz", None, "gx", None), P(None, "gz", None, "gx", None), P()),
        check_vma=False,
    )
```

```python
import functools
import math

import jax
import jax.numpy as jnp
import numpy as np
from jax import lax
from jax.experimental import pallas as pl
from jax.experimental.pallas import tpu as pltpu
from jax.sharding import PartitionSpec as P

SWEEPS = 3
POISSON = 4
SHIFTS = 8


viscosity = 0.4
shift_table = (0.6, 0.8, 1.0, 1.25, 1.6, 2.0, 2.5, 3.2)
chebyshev_weights = (1.0 / 1.9352976, 1.0 / 1.4752809, 1.0 / 0.8247191, 1.0 / 0.3647024)
highest = lax.Precision.HIGHEST


def step_kernel(
    sizes,
    shift_ref,
    cells_ref,
    given_factor,
    gain_ref,
    given_base,
    table_ref,
    scale_ref,
    natural,
    new_gain_ref,
    gram_ref,
    factor_ref,
    base_ref,
    solved_ref,
    fields,
    inverse,
    row_sends,
    row_halos,
    blocks,
    planes,
    rhs,
    modes,
    beside,
    pressure,
    pressure_row,
    pressure_halo,
    slots_z,
    slots_x,
    slots_y,
    mid,
    halo_send,
    halo_recv,
    turn_send,
    turn_recv,
    mode_send,
    mode_recv,
    sum_send,
    sum_recv,
):
    count_z, count_x, count_y = sizes
    count_gx = count_x * count_y
    components, span_cells, columns, stream_cells, normal_cells = given_factor.shape
    last_cell = stream_cells - 1
    cells = stream_cells * columns
    gx, gz = lax.axis_index("gx"), lax.axis_index("gz")
    here_x, here_y = gx % count_x, gx // count_x
    next_gx = ((gx + 1) % count_gx, gz)
    before_gx = ((gx + count_gx - 1) % count_gx, gz)
    next_gz = (gx, (gz + 1) % count_z)
    before_gz = (gx, (gz + count_z - 1) % count_z)
    shift = jnp.float32(shift_table[0])
    for entry in range(1, SHIFTS):
        shift = jnp.where(shift_ref[0] == entry, jnp.float32(shift_table[entry]), shift)

    odd = gx % 2
    turn = 1 - 2 * odd

    def mirrored(cell):
        return odd * last_cell + turn * cell

    plane_cell = mirrored(gz % stream_cells)
    plane_column = gz // stream_cells
    at_end = plane_cell // last_cell
    at_start = (last_cell - plane_cell) // last_cell
    plane_next = ((gx + at_end) % count_gx, gz + turn * (1 - at_end))
    plane_before = ((gx + count_gx - at_start) % count_gx, gz - turn * (1 - at_start))

    def low(cell):
        return jnp.where(gx + cell == 0, 0.0, 1.0)

    def high(cell):
        return jnp.where(count_gx - 1 - gx + last_cell - cell == 0, 0.0, 1.0)

    def partner(stage, offset):
        if stage == 0:
            return (gx, (gz + offset) % count_z)
        if stage == 1:
            return (here_y * count_x + (here_x + offset) % count_x, gz)
        return ((here_y + offset) % count_y * count_x + here_x, gz)

    def remote(src, dst, send, recv, device):
        return pltpu.make_async_remote_copy(
            src_ref=src,
            dst_ref=dst,
            send_sem=send,
            recv_sem=recv,
            device_id=device,
            device_id_type=pl.DeviceIdType.MESH,
        )

    def loop(first, end, act):
        def run(index, carry):
            act(index)
            return carry

        lax.fori_loop(first, end, run, 0)

    counts = (count_z, count_x, count_y)
    barrier = pltpu.get_barrier_semaphore()

    def greet(device):
        pl.semaphore_signal(barrier, inc=1, device_id=device, device_id_type=pl.DeviceIdType.MESH)

    for stage in range(3):
        loop(1, counts[stage], lambda offset, stage=stage: greet(partner(stage, offset)))
    greet(next_gx)
    greet(before_gx)

    rows = lax.broadcasted_iota(jnp.int32, (span_cells, normal_cells), 0)
    lanes = lax.broadcasted_iota(jnp.int32, (span_cells, normal_cells), 1)

    def normal_before(block):
        return jnp.where(lanes == 0, 0.0, pltpu.roll(block, 1, 1))

    def normal_after(block):
        return jnp.where(lanes == normal_cells - 1, 0.0, pltpu.roll(block, normal_cells - 1, 1))

    def span_before(block, halo):
        return jnp.where(rows == 0, halo, pltpu.roll(block, 1, 0))

    def span_after(block, halo):
        return jnp.where(rows == span_cells - 1, halo, pltpu.roll(block, span_cells - 1, 0))

    def halo_copies(level, part):
        moves = (
            (fields.at[level, part, stream_cells], fields.at[level, part, 0], next_gx),
            (fields.at[level, part, 1], fields.at[level, part, stream_cells + 1], before_gx),
            (row_sends.at[level, part, 0], row_halos.at[level, part, 0], next_gz),
            (row_sends.at[level, part, 1], row_halos.at[level, part, 1], before_gz),
        )
        sides = (0, 1, 2, 3) if level < SWEEPS else ((0,), (), (2,))[part]
        copies = []
        for side in sides:
            src, dst, device = moves[side]
            copies.append(
                remote(src, dst, halo_send.at[level, part, side], halo_recv.at[level, part, side], device)
            )
        return copies

    def keep(level, part, cell, column, block):
        index = cell * columns + column
        fields[level, part, cell + 1, column] = block
        row_sends[level, part, 0, index] = block[span_cells - 1 :]
        row_sends[level, part, 1, index] = block[:1]

    for cell in range(stream_cells):
        base_ref[cell] = given_base[:, cell, :]
        inverse[cell] = 1.0 / (shift + 6.0 * viscosity + base_ref[cell])
    for part in range(components):
        for cell in range(stream_cells):
            for column in range(columns):
                block = given_factor[part, :, column, cell, :]
                factor_ref[part, cell, column] = block
                keep(0, part, cell, column, -block * inverse[cell])
    pl.semaphore_wait(barrier, sum(counts) - 3 + 2)
    order = (0, 2, 1)
    for part in order:
        for copy in halo_copies(0, part):
            copy.start()
    for level in range(SWEEPS):
        for part in order:
            for copy in halo_copies(level, part):
                copy.wait()

            def sweep(cell, level=level, part=part):
                for column in range(columns):
                    index = cell * columns + column
                    block = fields[level, part, cell + 1, column]
                    behind = fields[level, part, cell, column] * low(cell)
                    around = behind + fields[level, part, cell + 2, column] * high(cell)
                    around = around + normal_before(block) + normal_after(block)
                    around = around + span_before(block, row_halos[level, part, 0, index])
                    around = around + span_after(block, row_halos[level, part, 1, index])
                    total = viscosity * around + base_ref[cell] * behind
                    total = total - factor_ref[part, cell, column]
                    keep(level + 1, part, cell, column, total * inverse[cell])

            loop(0, stream_cells, sweep)
            for copy in halo_copies(level + 1, part):
                copy.start()
    for part in range(components):
        for copy in halo_copies(SWEEPS, part):
            copy.wait()

    def spread(step):
        return count_z // 2 + step // 2 * (1 - 2 * (step % 2))

    def diverge(target):
        cell, column = mirrored(target % stream_cells), target // stream_cells
        index = cell * columns + column
        normal = fields[SWEEPS, 1, cell + 1, column]
        span = fields[SWEEPS, 2, cell + 1, column]
        total = 2.0 * (
            fields[SWEEPS, 0, cell + 1, column] - fields[SWEEPS, 0, cell, column] * low(cell)
        )
        total = total + (normal - normal_before(normal))
        return -(total + (span - span_before(span, row_halos[SWEEPS, 2, 0, index])))

    def gather_copy(step):
        offset = spread(step)
        device = partner(0, offset)
        return remote(
            blocks.at[device[1]], planes.at[gz], turn_send.at[0, offset], turn_recv.at[0, offset], device
        )

    def gather_start(step):
        target = partner(0, spread(step))[1]
        blocks[target] = diverge(target)
        gather_copy(step).start()

    loop(1, count_z, gather_start)
    planes[gz] = diverge(gz)
    loop(1, count_z, lambda step: gather_copy(step).wait())
    span_total = count_z * span_cells
    chunks = 4
    group = count_z // chunks
    height = span_total // chunks
    shape = (group, span_cells, normal_cells)

    def mode_copies(level, chunk):
        part = pl.ds(chunk * group, group)
        return [
            remote(
                modes.at[level, part],
                beside.at[level, side, part],
                mode_send.at[level, side, chunk],
                mode_recv.at[level, side, chunk],
                device,
            )
            for side, device in enumerate((plane_next, plane_before))
        ]

    whole = planes[...].reshape(span_total, normal_cells)
    for chunk in range(chunks):
        lines = slice(chunk * height, (chunk + 1) * height)
        spectrum = jnp.dot(
            table_ref[lines, :], whole, precision=highest, preferred_element_type=jnp.float32
        ) * scale_ref[lines, :]
        part = slice(chunk * group, (chunk + 1) * group)
        rhs[part] = spectrum.reshape(shape)
        modes[0, part] = (chebyshev_weights[0] * spectrum).reshape(shape)
        for copy in mode_copies(0, chunk):
            copy.start()

    plane_low, plane_high = 4.0 * low(plane_cell), 4.0 * high(plane_cell)
    for level in range(POISSON - 1):
        weight = chebyshev_weights[level + 1]
        for chunk in range(chunks):
            for copy in mode_copies(level, chunk):
                copy.wait()
            for index in range(chunk * group, (chunk + 1) * group):
                block = modes[level, index]
                around = plane_low * beside[level, 0, index] + plane_high * beside[level, 1, index]
                around = around + normal_before(block) + normal_after(block)
                scale = scale_ref[index * span_cells : (index + 1) * span_cells, :]
                modes[level + 1, index] = (1.0 - weight) * block + weight * (rhs[index] + scale * around)
            if level < POISSON - 2:
                for copy in mode_copies(level + 1, chunk):
                    copy.start()
    whole = modes[POISSON - 1].reshape(span_total, normal_cells)

    def scatter_copy(offset):
        device = partner(0, offset)
        return remote(
            blocks.at[device[1]],
            pressure.at[plane_cell, plane_column],
            turn_send.at[1, offset],
            turn_recv.at[1, offset],
            device,
        )

    for chunk in range(chunks):
        chosen = (gz // group + chunks // 2 + chunk) % chunks
        lines = pl.ds(pl.multiple_of(chosen * height, height), height)
        back = jnp.dot(table_ref[lines, :], whole, precision=highest, preferred_element_type=jnp.float32)
        blocks[pl.ds(chosen * group, group)] = back.reshape(shape)

        def scatter_start(member, chosen=chosen):
            target = chosen * group + member

            @pl.when(target != gz)
            def _():
                scatter_copy((target + count_z - gz) % count_z).start()

        loop(0, group, scatter_start)
    pressure[plane_cell, plane_column] = blocks[gz]
    loop(1, count_z, lambda offset: scatter_copy(offset).wait())

    for cell in range(stream_cells):
        for column in range(columns):
            pressure_row[cell * columns + column] = pressure[cell, column][:1]
    copies = (
        remote(pressure.at[0], pressure.at[stream_cells], mode_send.at[POISSON - 1, 0, 0], mode_recv.at[POISSON - 1, 0, 0], before_gx),
        remote(pressure_row, pressure_halo, mode_send.at[POISSON - 1, 1, 0], mode_recv.at[POISSON - 1, 1, 0], before_gz),
    )
    for copy in copies:
        copy.start()
    for copy in copies:
        copy.wait()

    pairs = [(i, j) for i in range(columns) for j in range(i, columns)]
    half = normal_cells // 2

    def finish(cell, sums):
        updated = []
        for column in range(columns):
            block = pressure[cell, column]
            gradient = (
                2.0 * (pressure[cell + 1, column] * high(cell) - block),
                normal_after(block) - block,
                span_after(block, pressure_halo[cell * columns + column]) - block,
            )
            updated.append([])
            for part in range(components):
                value = fields[SWEEPS, part, cell + 1, column] - gradient[part]
                solved_ref[part, cell, column] = value
                updated[column].append(factor_ref[part, cell, column] + 2.0 * shift * value)
        totals = []
        for total, (i, j) in zip(sums, pairs):
            product = updated[i][0] * updated[j][0]
            for part in range(1, components):
                product = product + updated[i][part] * updated[j][part]
            product = product[:, :half] + product[:, half:]
            totals.append(total + product[:8] + product[8:])
        return tuple(totals)

    zero = jnp.zeros((8, half), jnp.float32)
    sums = lax.fori_loop(0, stream_cells, finish, (zero,) * len(pairs))
    tile_lanes = lax.broadcasted_iota(jnp.int32, (1, 128), 1)
    tile = jnp.zeros((1, 128), jnp.float32)

    def put(tile, row, lane, value):
        return jnp.where(tile_lanes == row * columns + lane, value, tile)

    for total, (i, j) in zip(sums, pairs):
        value = jnp.sum(jnp.sum(total, axis=1, keepdims=True), axis=0, keepdims=True)
        tile = put(tile, i, j, value)
        if i != j:
            tile = put(tile, j, i, value)
    line_lanes = lax.broadcasted_iota(jnp.int32, (1, normal_cells), 1)
    for sensor in range(cells_ref.shape[0]):
        part = jnp.clip(cells_ref[sensor, 0], 0, components - 1)
        span = cells_ref[sensor, 1] - gz * span_cells
        stream = cells_ref[sensor, 2] - gx * stream_cells
        inside = (span >= 0) & (span < span_cells) & (stream >= 0) & (stream < stream_cells)
        span = jnp.clip(span, 0, span_cells - 1)
        stream = jnp.clip(stream, 0, stream_cells - 1)
        chosen = (line_lanes == cells_ref[sensor, 3]) & inside
        for column in range(columns):
            line = solved_ref[part, stream, column, pl.ds(span, 1), :]
            value = jnp.sum(jnp.where(chosen, line, 0.0), axis=1, keepdims=True)
            tile = put(tile, columns + sensor, column, value)
    mid[0] = tile
    places = (gz, here_x, here_y)
    bases = (0, count_z, count_z + count_x)
    for stage, slots in enumerate((slots_z, slots_x, slots_y)):
        def sum_copy(offset, stage=stage, slots=slots):
            index = bases[stage] + offset
            return remote(
                mid.at[stage], slots.at[places[stage]], sum_send.at[index], sum_recv.at[index], partner(stage, offset)
            )

        loop(1, counts[stage], lambda offset, sum_copy=sum_copy: sum_copy(offset).start())
        if stage == 0:
            for part in range(components):
                for cell in range(stream_cells):
                    for column in range(columns):
                        block = solved_ref[part, cell, column] * (2.0 * shift)
                        natural[part, :, column, cell, :] = block
        slots[places[stage]] = mid[stage]
        loop(1, counts[stage], lambda offset, sum_copy=sum_copy: sum_copy(offset).wait())
        total = slots[0]
        for place in range(1, counts[stage]):
            total = total + slots[place]
        if stage < 2:
            mid[stage + 1] = total
        else:
            def entry(row, lane):
                place = row * columns + lane
                return total[:, place : place + 1]

            gram_rows = lax.broadcasted_iota(jnp.int32, (columns, columns), 0)
            gram_lanes = lax.broadcasted_iota(jnp.int32, (columns, columns), 1)
            gram = jnp.zeros((columns, columns), jnp.float32)
            for i in range(columns):
                for j in range(columns):
                    gram = jnp.where((gram_rows == i) & (gram_lanes == j), entry(i, j), gram)
            all_cells = components * stream_cells * count_gx * normal_cells * span_cells * count_z
            gram_ref[...] = gram * (1.0 / all_cells)
            readout = [[entry(columns + i, j) for j in range(columns)] for i in range(columns)]

            def gain(span):
                for part in range(components):
                    steps = [natural[part, span, j] for j in range(columns)]
                    for i in range(columns):
                        value = gain_ref[part, span, i]
                        for j in range(columns):
                            value = value + steps[j] * readout[i][j]
                        new_gain_ref[part, span, i] = value

            loop(0, span_cells, gain)


def hartley_table(span_total):
    index = np.arange(span_total)
    angles = 2.0 * math.pi * (index[:, None] * index[None, :] % span_total) / span_total
    return ((np.cos(angles) + np.sin(angles)) / math.sqrt(span_total)).astype(np.float32)


def mode_scale(span_total, normal_cells):
    wavenumber = 2.0 * math.pi * np.arange(span_total) / span_total
    diagonal = 10.0 + (2.0 - 2.0 * np.cos(wavenumber))
    return np.repeat((1.0 / diagonal).astype(np.float32)[:, None], normal_cells, axis=1)


def solve(factor, gain, base_flow, shift_index, sensor_cells, sizes):
    count_z, count_x, count_y = sizes
    components, span_cells, columns, stream_cells, normal_cells = factor.shape
    cells = stream_cells * columns
    span_total = count_z * span_cells
    vmem = pl.BlockSpec(memory_space=pltpu.VMEM)
    smem = pl.BlockSpec(memory_space=pltpu.SMEM)
    f32 = jnp.float32
    group = (count_z, span_cells, normal_cells)
    turned = (components, stream_cells, columns, span_cells, normal_cells)
    dma = pltpu.SemaphoreType.DMA
    return pl.pallas_call(
        functools.partial(step_kernel, sizes),
        out_shape=(
            jax.ShapeDtypeStruct(factor.shape, f32),
            jax.ShapeDtypeStruct(gain.shape, f32),
            jax.ShapeDtypeStruct((columns, columns), f32),
        ),
        in_specs=[smem, smem, vmem, vmem, vmem, vmem, vmem],
        out_specs=(vmem, vmem, vmem),
        scratch_shapes=[
            pltpu.VMEM(turned, f32),
            pltpu.VMEM((stream_cells, span_cells, normal_cells), f32),
            pltpu.VMEM(turned, f32),
            pltpu.VMEM((SWEEPS + 1, components, stream_cells + 2, columns, span_cells, normal_cells), f32),
            pltpu.VMEM((stream_cells, span_cells, normal_cells), f32),
            pltpu.VMEM((SWEEPS + 1, components, 2, cells, 1, normal_cells), f32),
            pltpu.VMEM((SWEEPS + 1, components, 2, cells, 1, normal_cells), f32),
            pltpu.VMEM(group, f32),
            pltpu.VMEM(group, f32),
            pltpu.VMEM(group, f32),
            pltpu.VMEM((POISSON,) + group, f32),
            pltpu.VMEM((POISSON - 1, 2) + group, f32),
            pltpu.VMEM((stream_cells + 1, columns, span_cells, normal_cells), f32),
            pltpu.VMEM((cells, 1, normal_cells), f32),
            pltpu.VMEM((cells, 1, normal_cells), f32),
        ]
        + [pltpu.VMEM((size, 1, 128), f32) for size in sizes]
        + [
            pltpu.VMEM((3, 1, 128), f32),
            dma((SWEEPS + 1, components, 4)),
            dma((SWEEPS + 1, components, 4)),
            dma((2, count_z)),
            dma((2, count_z)),
            dma((POISSON, 2, 4)),
            dma((POISSON, 2, 4)),
            dma((sum(sizes),)),
            dma((sum(sizes),)),
        ],
        compiler_params=pltpu.CompilerParams(collective_id=0, has_side_effects=True),
        name="solve",
    )(
        shift_index,
        sensor_cells,
        factor,
        gain,
        base_flow,
        jnp.asarray(hartley_table(span_total)),
        jnp.asarray(mode_scale(span_total, normal_cells)),
    )


def shards(factor, gain, base_flow, shift_index, sensor_cells):
    count_gx, count_z = lax.axis_size("gx"), lax.axis_size("gz")
    count_x = 4 if count_gx % 4 == 0 else count_gx
    sizes = (count_z, count_x, count_gx // count_x)
    step, new_gain, gram = solve(factor, gain, base_flow, shift_index, sensor_cells, sizes)
    return (factor + step, new_gain, gram)


def solution(mesh):
    placed = (
        P(None, "gz", None, "gx", None),
        P(None, "gz", None, "gx", None),
        P("gz", "gx", None),
        P(),
        P(),
    )
    return jax.shard_map(
        shards,
        mesh=mesh,
        in_specs=placed,
        out_specs=(P(None, "gz", None, "gx", None), P(None, "gz", None, "gx", None), P()),
        check_vma=False,
    )
```

```python
import functools
import math

import jax
import jax.numpy as jnp
import numpy as np
from jax import lax
from jax.experimental import pallas as pl
from jax.experimental.pallas import tpu as pltpu
from jax.sharding import PartitionSpec as P

SWEEPS = 3
POISSON = 4
SHIFTS = 8


viscosity = 0.4
shift_table = (0.6, 0.8, 1.0, 1.25, 1.6, 2.0, 2.5, 3.2)
chebyshev_weights = (1.0 / 1.9352976, 1.0 / 1.4752809, 1.0 / 0.8247191, 1.0 / 0.3647024)
highest = lax.Precision.HIGHEST


def step_kernel(
    sizes,
    shift_ref,
    cells_ref,
    given_factor,
    far_gain,
    given_base,
    far_table,
    far_scale,
    natural,
    new_gain_ref,
    gram_ref,
    factor_ref,
    base_ref,
    solved_ref,
    gain_ref,
    table_ref,
    scale_ref,
    near,
    fields,
    inverse,
    row_sends,
    row_halos,
    blocks,
    planes,
    rhs,
    modes,
    beside,
    pressure,
    pressure_row,
    pressure_halo,
    slots_z,
    slots_x,
    slots_y,
    mid,
    halo_send,
    halo_recv,
    turn_send,
    turn_recv,
    mode_send,
    mode_recv,
    sum_send,
    sum_recv,
):
    count_z, count_x, count_y = sizes
    count_gx = count_x * count_y
    components, span_cells, columns, stream_cells, normal_cells = given_factor.shape
    last_cell = stream_cells - 1
    cells = stream_cells * columns
    gx, gz = lax.axis_index("gx"), lax.axis_index("gz")
    here_x, here_y = gx % count_x, gx // count_x
    next_gx = ((gx + 1) % count_gx, gz)
    before_gx = ((gx + count_gx - 1) % count_gx, gz)
    next_gz = (gx, (gz + 1) % count_z)
    before_gz = (gx, (gz + count_z - 1) % count_z)
    shift = jnp.float32(shift_table[0])
    for entry in range(1, SHIFTS):
        shift = jnp.where(shift_ref[0] == entry, jnp.float32(shift_table[entry]), shift)

    odd = gx % 2
    turn = 1 - 2 * odd

    def mirrored(cell):
        return odd * last_cell + turn * cell

    plane_cell = mirrored(gz % stream_cells)
    plane_column = gz // stream_cells
    at_end = plane_cell // last_cell
    at_start = (last_cell - plane_cell) // last_cell
    plane_next = ((gx + at_end) % count_gx, gz + turn * (1 - at_end))
    plane_before = ((gx + count_gx - at_start) % count_gx, gz - turn * (1 - at_start))

    def low(cell):
        return jnp.where(gx + cell == 0, 0.0, 1.0)

    def high(cell):
        return jnp.where(count_gx - 1 - gx + last_cell - cell == 0, 0.0, 1.0)

    def partner(stage, offset):
        if stage == 0:
            return (gx, (gz + offset) % count_z)
        if stage == 1:
            return (here_y * count_x + (here_x + offset) % count_x, gz)
        return ((here_y + offset) % count_y * count_x + here_x, gz)

    def remote(src, dst, send, recv, device):
        return pltpu.make_async_remote_copy(
            src_ref=src,
            dst_ref=dst,
            send_sem=send,
            recv_sem=recv,
            device_id=device,
            device_id_type=pl.DeviceIdType.MESH,
        )

    def loop(first, end, act):
        def run(index, carry):
            act(index)
            return carry

        lax.fori_loop(first, end, run, 0)

    loads = [
        pltpu.make_async_copy(src, dst, near.at[place])
        for place, (src, dst) in enumerate(
            ((far_table, table_ref), (far_scale, scale_ref), (far_gain, gain_ref))
        )
    ]
    for load in loads:
        load.start()
    counts = (count_z, count_x, count_y)
    barrier = pltpu.get_barrier_semaphore()

    def greet(device):
        pl.semaphore_signal(barrier, inc=1, device_id=device, device_id_type=pl.DeviceIdType.MESH)

    for stage in range(3):
        loop(1, counts[stage], lambda offset, stage=stage: greet(partner(stage, offset)))
    greet(next_gx)
    greet(before_gx)

    rows = lax.broadcasted_iota(jnp.int32, (span_cells, normal_cells), 0)
    lanes = lax.broadcasted_iota(jnp.int32, (span_cells, normal_cells), 1)

    def normal_before(block):
        return jnp.where(lanes == 0, 0.0, pltpu.roll(block, 1, 1))

    def normal_after(block):
        return jnp.where(lanes == normal_cells - 1, 0.0, pltpu.roll(block, normal_cells - 1, 1))

    def span_before(block, halo):
        return jnp.where(rows == 0, halo, pltpu.roll(block, 1, 0))

    def span_after(block, halo):
        return jnp.where(rows == span_cells - 1, halo, pltpu.roll(block, span_cells - 1, 0))

    def halo_copies(level, part):
        moves = (
            (fields.at[level, part, stream_cells], fields.at[level, part, 0], next_gx),
            (fields.at[level, part, 1], fields.at[level, part, stream_cells + 1], before_gx),
            (row_sends.at[level, part, 0], row_halos.at[level, part, 0], next_gz),
            (row_sends.at[level, part, 1], row_halos.at[level, part, 1], before_gz),
        )
        sides = (0, 1, 2, 3) if level < SWEEPS else ((0,), (), (2,))[part]
        copies = []
        for side in sides:
            src, dst, device = moves[side]
            copies.append(
                remote(src, dst, halo_send.at[level, part, side], halo_recv.at[level, part, side], device)
            )
        return copies

    def keep(level, part, cell, column, block):
        index = cell * columns + column
        fields[level, part, cell + 1, column] = block
        row_sends[level, part, 0, index] = block[span_cells - 1 :]
        row_sends[level, part, 1, index] = block[:1]

    for cell in range(stream_cells):
        base_ref[cell] = given_base[:, cell, :]
        inverse[cell] = 1.0 / (shift + 6.0 * viscosity + base_ref[cell])
    for part in range(components):
        for cell in range(stream_cells):
            for column in range(columns):
                block = given_factor[part, :, column, cell, :]
                factor_ref[part, cell, column] = block
                keep(0, part, cell, column, -block * inverse[cell])
    pl.semaphore_wait(barrier, sum(counts) - 3 + 2)
    order = (0, 2, 1)
    for part in order:
        for copy in halo_copies(0, part):
            copy.start()
    for level in range(SWEEPS):
        for part in order:
            for copy in halo_copies(level, part):
                copy.wait()

            def sweep(cell, level=level, part=part):
                for column in range(columns):
                    index = cell * columns + column
                    block = fields[level, part, cell + 1, column]
                    behind = fields[level, part, cell, column] * low(cell)
                    around = behind + fields[level, part, cell + 2, column] * high(cell)
                    around = around + normal_before(block) + normal_after(block)
                    around = around + span_before(block, row_halos[level, part, 0, index])
                    around = around + span_after(block, row_halos[level, part, 1, index])
                    total = viscosity * around + base_ref[cell] * behind
                    total = total - factor_ref[part, cell, column]
                    keep(level + 1, part, cell, column, total * inverse[cell])

            loop(0, stream_cells, sweep)
            for copy in halo_copies(level + 1, part):
                copy.start()
    for part in range(components):
        for copy in halo_copies(SWEEPS, part):
            copy.wait()

    def spread(step):
        return count_z // 2 + step // 2 * (1 - 2 * (step % 2))

    def diverge(target):
        cell, column = mirrored(target % stream_cells), target // stream_cells
        index = cell * columns + column
        normal = fields[SWEEPS, 1, cell + 1, column]
        span = fields[SWEEPS, 2, cell + 1, column]
        total = 2.0 * (
            fields[SWEEPS, 0, cell + 1, column] - fields[SWEEPS, 0, cell, column] * low(cell)
        )
        total = total + (normal - normal_before(normal))
        return -(total + (span - span_before(span, row_halos[SWEEPS, 2, 0, index])))

    def gather_copy(step):
        offset = spread(step)
        device = partner(0, offset)
        return remote(
            blocks.at[device[1]], planes.at[gz], turn_send.at[0, offset], turn_recv.at[0, offset], device
        )

    def gather_start(step):
        target = partner(0, spread(step))[1]
        blocks[target] = diverge(target)
        gather_copy(step).start()

    loop(1, count_z, gather_start)
    planes[gz] = diverge(gz)
    loop(1, count_z, lambda step: gather_copy(step).wait())
    span_total = count_z * span_cells
    chunks = 4
    group = count_z // chunks
    height = span_total // chunks
    shape = (group, span_cells, normal_cells)

    def mode_copies(level, chunk):
        part = pl.ds(chunk * group, group)
        return [
            remote(
                modes.at[level, part],
                beside.at[level, side, part],
                mode_send.at[level, side, chunk],
                mode_recv.at[level, side, chunk],
                device,
            )
            for side, device in enumerate((plane_next, plane_before))
        ]

    loads[0].wait()
    loads[1].wait()
    whole = planes[...].reshape(span_total, normal_cells)
    for chunk in range(chunks):
        lines = slice(chunk * height, (chunk + 1) * height)
        spectrum = jnp.dot(
            table_ref[lines, :], whole, precision=highest, preferred_element_type=jnp.float32
        ) * scale_ref[lines, :]
        part = slice(chunk * group, (chunk + 1) * group)
        rhs[part] = spectrum.reshape(shape)
        modes[0, part] = (chebyshev_weights[0] * spectrum).reshape(shape)
        for copy in mode_copies(0, chunk):
            copy.start()

    plane_low, plane_high = 4.0 * low(plane_cell), 4.0 * high(plane_cell)
    for level in range(POISSON - 1):
        weight = chebyshev_weights[level + 1]
        for chunk in range(chunks):
            for copy in mode_copies(level, chunk):
                copy.wait()
            for index in range(chunk * group, (chunk + 1) * group):
                block = modes[level, index]
                around = plane_low * beside[level, 0, index] + plane_high * beside[level, 1, index]
                around = around + normal_before(block) + normal_after(block)
                scale = scale_ref[index * span_cells : (index + 1) * span_cells, :]
                modes[level + 1, index] = (1.0 - weight) * block + weight * (rhs[index] + scale * around)
            if level < POISSON - 2:
                for copy in mode_copies(level + 1, chunk):
                    copy.start()
    whole = modes[POISSON - 1].reshape(span_total, normal_cells)

    def scatter_copy(offset):
        device = partner(0, offset)
        return remote(
            blocks.at[device[1]],
            pressure.at[plane_cell, plane_column],
            turn_send.at[1, offset],
            turn_recv.at[1, offset],
            device,
        )

    for chunk in range(chunks):
        chosen = (gz // group + chunks // 2 + chunk) % chunks
        lines = pl.ds(pl.multiple_of(chosen * height, height), height)
        back = jnp.dot(table_ref[lines, :], whole, precision=highest, preferred_element_type=jnp.float32)
        blocks[pl.ds(chosen * group, group)] = back.reshape(shape)

        def scatter_start(member, chosen=chosen):
            target = chosen * group + member

            @pl.when(target != gz)
            def _():
                scatter_copy((target + count_z - gz) % count_z).start()

        loop(0, group, scatter_start)
    pressure[plane_cell, plane_column] = blocks[gz]
    loop(1, count_z, lambda offset: scatter_copy(offset).wait())

    for cell in range(stream_cells):
        for column in range(columns):
            pressure_row[cell * columns + column] = pressure[cell, column][:1]
    copies = (
        remote(pressure.at[0], pressure.at[stream_cells], mode_send.at[POISSON - 1, 0, 0], mode_recv.at[POISSON - 1, 0, 0], before_gx),
        remote(pressure_row, pressure_halo, mode_send.at[POISSON - 1, 1, 0], mode_recv.at[POISSON - 1, 1, 0], before_gz),
    )
    for copy in copies:
        copy.start()
    for copy in copies:
        copy.wait()

    pairs = [(i, j) for i in range(columns) for j in range(i, columns)]
    half = normal_cells // 2

    def finish(cell, sums):
        updated = []
        for column in range(columns):
            block = pressure[cell, column]
            gradient = (
                2.0 * (pressure[cell + 1, column] * high(cell) - block),
                normal_after(block) - block,
                span_after(block, pressure_halo[cell * columns + column]) - block,
            )
            updated.append([])
            for part in range(components):
                value = fields[SWEEPS, part, cell + 1, column] - gradient[part]
                solved_ref[part, cell, column] = value
                updated[column].append(factor_ref[part, cell, column] + 2.0 * shift * value)
        totals = []
        for total, (i, j) in zip(sums, pairs):
            product = updated[i][0] * updated[j][0]
            for part in range(1, components):
                product = product + updated[i][part] * updated[j][part]
            product = product[:, :half] + product[:, half:]
            totals.append(total + product[:8] + product[8:])
        return tuple(totals)

    zero = jnp.zeros((8, half), jnp.float32)
    sums = lax.fori_loop(0, stream_cells, finish, (zero,) * len(pairs))
    tile_lanes = lax.broadcasted_iota(jnp.int32, (1, 128), 1)
    tile = jnp.zeros((1, 128), jnp.float32)

    def put(tile, row, lane, value):
        return jnp.where(tile_lanes == row * columns + lane, value, tile)

    for total, (i, j) in zip(sums, pairs):
        value = jnp.sum(jnp.sum(total, axis=1, keepdims=True), axis=0, keepdims=True)
        tile = put(tile, i, j, value)
        if i != j:
            tile = put(tile, j, i, value)
    line_lanes = lax.broadcasted_iota(jnp.int32, (1, normal_cells), 1)
    for sensor in range(cells_ref.shape[0]):
        part = jnp.clip(cells_ref[sensor, 0], 0, components - 1)
        span = cells_ref[sensor, 1] - gz * span_cells
        stream = cells_ref[sensor, 2] - gx * stream_cells
        inside = (span >= 0) & (span < span_cells) & (stream >= 0) & (stream < stream_cells)
        span = jnp.clip(span, 0, span_cells - 1)
        stream = jnp.clip(stream, 0, stream_cells - 1)
        chosen = (line_lanes == cells_ref[sensor, 3]) & inside
        for column in range(columns):
            line = solved_ref[part, stream, column, pl.ds(span, 1), :]
            value = jnp.sum(jnp.where(chosen, line, 0.0), axis=1, keepdims=True)
            tile = put(tile, columns + sensor, column, value)
    mid[0] = tile
    places = (gz, here_x, here_y)
    bases = (0, count_z, count_z + count_x)
    for stage, slots in enumerate((slots_z, slots_x, slots_y)):
        def sum_copy(offset, stage=stage, slots=slots):
            index = bases[stage] + offset
            return remote(
                mid.at[stage], slots.at[places[stage]], sum_send.at[index], sum_recv.at[index], partner(stage, offset)
            )

        loop(1, counts[stage], lambda offset, sum_copy=sum_copy: sum_copy(offset).start())
        if stage == 0:
            for part in range(components):
                for cell in range(stream_cells):
                    for column in range(columns):
                        block = solved_ref[part, cell, column] * (2.0 * shift)
                        natural[part, :, column, cell, :] = block
        slots[places[stage]] = mid[stage]
        loop(1, counts[stage], lambda offset, sum_copy=sum_copy: sum_copy(offset).wait())
        total = slots[0]
        for place in range(1, counts[stage]):
            total = total + slots[place]
        if stage < 2:
            mid[stage + 1] = total
        else:
            def entry(row, lane):
                place = row * columns + lane
                return total[:, place : place + 1]

            gram_rows = lax.broadcasted_iota(jnp.int32, (columns, columns), 0)
            gram_lanes = lax.broadcasted_iota(jnp.int32, (columns, columns), 1)
            gram = jnp.zeros((columns, columns), jnp.float32)
            for i in range(columns):
                for j in range(columns):
                    gram = jnp.where((gram_rows == i) & (gram_lanes == j), entry(i, j), gram)
            all_cells = components * stream_cells * count_gx * normal_cells * span_cells * count_z
            gram_ref[...] = gram * (1.0 / all_cells)
            readout = [[entry(columns + i, j) for j in range(columns)] for i in range(columns)]

            loads[2].wait()

            def gain(span):
                for part in range(components):
                    steps = [natural[part, span, j] for j in range(columns)]
                    for i in range(columns):
                        value = gain_ref[part, span, i]
                        for j in range(columns):
                            value = value + steps[j] * readout[i][j]
                        new_gain_ref[part, span, i] = value

            loop(0, span_cells, gain)


def hartley_table(span_total):
    index = np.arange(span_total)
    angles = 2.0 * math.pi * (index[:, None] * index[None, :] % span_total) / span_total
    return ((np.cos(angles) + np.sin(angles)) / math.sqrt(span_total)).astype(np.float32)


def mode_scale(span_total, normal_cells):
    wavenumber = 2.0 * math.pi * np.arange(span_total) / span_total
    diagonal = 10.0 + (2.0 - 2.0 * np.cos(wavenumber))
    return np.repeat((1.0 / diagonal).astype(np.float32)[:, None], normal_cells, axis=1)


def solve(factor, gain, base_flow, shift_index, sensor_cells, sizes):
    count_z, count_x, count_y = sizes
    components, span_cells, columns, stream_cells, normal_cells = factor.shape
    cells = stream_cells * columns
    span_total = count_z * span_cells
    vmem = pl.BlockSpec(memory_space=pltpu.VMEM)
    smem = pl.BlockSpec(memory_space=pltpu.SMEM)
    far = pl.BlockSpec(memory_space=pl.ANY)
    f32 = jnp.float32
    group = (count_z, span_cells, normal_cells)
    turned = (components, stream_cells, columns, span_cells, normal_cells)
    dma = pltpu.SemaphoreType.DMA
    return pl.pallas_call(
        functools.partial(step_kernel, sizes),
        out_shape=(
            jax.ShapeDtypeStruct(factor.shape, f32),
            jax.ShapeDtypeStruct(gain.shape, f32),
            jax.ShapeDtypeStruct((columns, columns), f32),
        ),
        in_specs=[smem, smem, vmem, far, vmem, far, far],
        out_specs=(vmem, vmem, vmem),
        scratch_shapes=[
            pltpu.VMEM(turned, f32),
            pltpu.VMEM((stream_cells, span_cells, normal_cells), f32),
            pltpu.VMEM(turned, f32),
            pltpu.VMEM(gain.shape, f32),
            pltpu.VMEM((span_total, span_total), f32),
            pltpu.VMEM((span_total, normal_cells), f32),
            dma((3,)),
            pltpu.VMEM((SWEEPS + 1, components, stream_cells + 2, columns, span_cells, normal_cells), f32),
            pltpu.VMEM((stream_cells, span_cells, normal_cells), f32),
            pltpu.VMEM((SWEEPS + 1, components, 2, cells, 1, normal_cells), f32),
            pltpu.VMEM((SWEEPS + 1, components, 2, cells, 1, normal_cells), f32),
            pltpu.VMEM(group, f32),
            pltpu.VMEM(group, f32),
            pltpu.VMEM(group, f32),
            pltpu.VMEM((POISSON,) + group, f32),
            pltpu.VMEM((POISSON - 1, 2) + group, f32),
            pltpu.VMEM((stream_cells + 1, columns, span_cells, normal_cells), f32),
            pltpu.VMEM((cells, 1, normal_cells), f32),
            pltpu.VMEM((cells, 1, normal_cells), f32),
        ]
        + [pltpu.VMEM((size, 1, 128), f32) for size in sizes]
        + [
            pltpu.VMEM((3, 1, 128), f32),
            dma((SWEEPS + 1, components, 4)),
            dma((SWEEPS + 1, components, 4)),
            dma((2, count_z)),
            dma((2, count_z)),
            dma((POISSON, 2, 4)),
            dma((POISSON, 2, 4)),
            dma((sum(sizes),)),
            dma((sum(sizes),)),
        ],
        compiler_params=pltpu.CompilerParams(collective_id=0, has_side_effects=True),
        name="solve",
    )(
        shift_index,
        sensor_cells,
        factor,
        gain,
        base_flow,
        jnp.asarray(hartley_table(span_total)),
        jnp.asarray(mode_scale(span_total, normal_cells)),
    )


def shards(factor, gain, base_flow, shift_index, sensor_cells):
    count_gx, count_z = lax.axis_size("gx"), lax.axis_size("gz")
    count_x = 4 if count_gx % 4 == 0 else count_gx
    sizes = (count_z, count_x, count_gx // count_x)
    step, new_gain, gram = solve(factor, gain, base_flow, shift_index, sensor_cells, sizes)
    return (factor + step, new_gain, gram)


def solution(mesh):
    placed = (
        P(None, "gz", None, "gx", None),
        P(None, "gz", None, "gx", None),
        P("gz", "gx", None),
        P(),
        P(),
    )
    return jax.shard_map(
        shards,
        mesh=mesh,
        in_specs=placed,
        out_specs=(P(None, "gz", None, "gx", None), P(None, "gz", None, "gx", None), P()),
        check_vma=False,
    )
```
